256 devices in a mesh: blk: 64 (over y, z, x_hi), bin: 4 (over x_lo, core).
Axes of the slice: x: 4 (x_hi: 2, x_lo: 2; x = x_hi * 2 + x_lo), y: 4, z: 8, core: 2. Of those that a mesh axis runs over, the one named last changes fastest.
Arguments:
- spectrum: float32 [64, 8, 12, 512, 128], P('bin', None, None, 'blk'), may hold values from 0.05 to 2
- wind: float32 [8, 12, 128], replicated, may hold values from -12 to 12
- fall_speed: float32 [64], P('bin'), may hold values from 0.1 to 10
- collection: bfloat16 [64, 64, 64], P(None, None, 'bin'), may hold values from -0.09375 to 0.09375
- act_order: int32 [64, 8], P('blk'), may hold values from 0 to 7, each once within a row
- act_count: int32 [64], P('blk'), may hold values from 1 to 4, as said below
Outputs:
- updated: float32 [64, 8, 12, 512, 128], P('bin', None, None, 'blk')
The draws below stay inside these ranges and needn't reach their ends.
Inputs may be any that keep to these rules, and one draw needn't show every extreme that they name: `act_order`: each row names every block row once; the active ones are its first act_count entries. `act_count`: some column holds exactly half of 8 active blocks.
All inputs are finite; a program needn't handle non-finite values.
Results may differ from the reference program's by a relative error of at most 0.0055.
Values may be sent and summed in bfloat16 or wider, within the bound.
A program may use at most 128 MiB of HBM per device.

```python
import math
import jax
import jax.numpy as jnp
from jax import lax

NB = 64
SLOTS = 8
NZ = 12
BX = 8
BY = 128
NX = 512
N_BLK = 64


def draw_act_count(key, part):
    first_key, second_key = jax.random.split(jax.random.fold_in(key, 7))
    counts = jax.random.randint(first_key, (N_BLK,), 1, SLOTS // 2 + 1)
    chosen = jax.random.randint(second_key, (), 0, N_BLK)
    return jnp.where(jnp.arange(N_BLK) == chosen, SLOTS // 2, counts).astype(jnp.int32)


def steps_of(own_key, extent, pieces, smallest, top_value):
    factor_of = 1.0
    for position, blocks in pieces:
        draws = jax.random.uniform(jax.random.fold_in(jax.random.fold_in(own_key, 6), position), (blocks,), jnp.float32, smallest / len(pieces), top_value / len(pieces))
        factor_of = factor_of * jnp.repeat(jnp.exp(draws), extent[position] // blocks).reshape((-1,) + (1,) * (len(extent) - 1 - position))
    return factor_of


def noise(key, extent, scale, limit, cuts=(), kind=jnp.bfloat16):
    values = jax.random.normal(key, extent, jnp.float32) * scale
    if len(cuts) > 0:
        values = steps_of(key, extent, cuts, -0.22, 0.18) * values
    return jnp.clip(values, min=-limit, max=limit).astype(kind)


def setup_inputs(seed: int = 0) -> dict:
    key_of = jax.random.split(jax.random.key(seed), 7)
    return {
        "spectrum": jnp.clip(jnp.exp(math.log(2.0) - 3.6888794 * jax.random.uniform(key_of[0], (NB, SLOTS, NZ, NX, BY), jnp.float32) ** steps_of(key_of[0], (NB, SLOTS, NZ, NX, BY), ((0, 4), (3, 64)), -0.2, 0.2)), 0.05, 2.0),
        "wind": jnp.clip(jax.random.uniform(key_of[1], (SLOTS, NZ, BY), jnp.float32, -12.0, 12.0), -12.0, 12.0),
        "fall_speed": jnp.clip(jnp.exp(math.log(10.0) - 4.6051702 * jax.random.uniform(key_of[2], (NB,), jnp.float32) ** steps_of(key_of[2], (NB,), ((0, 4),), -0.2, 0.2)), 0.1, 10.0),
        "collection": noise(key_of[3], (NB, NB, NB), (NB * NB) ** -0.5, 0.09375, ((2, 4),)),
        "act_order": jax.vmap(lambda own: jax.random.permutation(own, SLOTS))(jax.random.split(key_of[4], N_BLK)).reshape((N_BLK, SLOTS)).astype(jnp.int32),
        "act_count": draw_act_count(jax.random.fold_in(key_of[6], 71), 0),
    }


weno_eps = 1e-6
courant = 0.04
time_step = 2.0


def reconstruct(first, second, third, fourth, fifth):
    cand_left = (2.0 * first - 7.0 * second + 11.0 * third) / 6.0
    cand_mid = (-second + 5.0 * third + 2.0 * fourth) / 6.0
    cand_right = (2.0 * third + 5.0 * fourth - fifth) / 6.0
    smooth_left = 13.0 / 12.0 * (first - 2.0 * second + third) ** 2 + 0.25 * (first - 4.0 * second + 3.0 * third) ** 2
    smooth_mid = 13.0 / 12.0 * (second - 2.0 * third + fourth) ** 2 + 0.25 * (second - fourth) ** 2
    smooth_right = 13.0 / 12.0 * (third - 2.0 * fourth + fifth) ** 2 + 0.25 * (3.0 * third - 4.0 * fourth + fifth) ** 2
    weight_left = 0.1 / (weno_eps + smooth_left) ** 2
    weight_mid = 0.6 / (weno_eps + smooth_mid) ** 2
    weight_right = 0.3 / (weno_eps + smooth_right) ** 2
    total = weight_left + weight_mid + weight_right
    return (weight_left * cand_left + weight_mid * cand_mid + weight_right * cand_right) / total


def advect(padded, field, wind):
    width = field.shape[3]

    def window(offset):
        return lax.slice_in_dim(padded, offset, offset + width + 1, axis=3)

    upwind_pos = reconstruct(window(0), window(1), window(2), window(3), window(4))
    upwind_neg = reconstruct(window(5), window(4), window(3), window(2), window(1))
    speed = wind[None, :, :, None, :]
    flux = jnp.where(speed > 0, speed * upwind_pos, speed * upwind_neg)
    return field - courant * (flux[:, :, :, 1:, :] - flux[:, :, :, :-1, :])


def sediment(field, fall_speed):
    above = jnp.concatenate([field[:, :, 1:], jnp.zeros_like(field[:, :, :1])], axis=2)
    return field - courant * fall_speed[:, None, None, None, None] * (field - above)


def reference(spectrum, wind, fall_speed, collection, act_order, act_count):
    padded = jnp.pad(spectrum, ((0, 0), (0, 0), (0, 0), (3, 3), (0, 0)))
    advected = advect(padded, spectrum, wind)
    settled = sediment(advected, fall_speed)
    columns = act_count.shape[0]
    capacity = SLOTS // 2
    blocks = settled.reshape(NB, SLOTS, NZ, columns, BX, BY)
    table = collection.reshape(NB, NB * NB)
    slot_ids = jnp.arange(SLOTS, dtype=jnp.int32)

    def one_column(column):
        update = jnp.zeros((NB, SLOTS, NZ, BX, BY), settled.dtype)
        for entry in range(capacity):
            slot = act_order[column, entry]
            block = blocks[:, slot, :, column]
            cells = block.reshape(NB, NZ * BX * BY).T.astype(jnp.bfloat16)
            inner = jnp.dot(cells, table, preferred_element_type=jnp.float32).astype(jnp.bfloat16)
            inner = inner.reshape(NZ * BX * BY, NB, NB)
            tendency = jnp.einsum("ci,cik->ck", cells.astype(jnp.float32), inner.astype(jnp.float32))
            tendency = tendency.T.reshape(NB, NZ, BX, BY)
            chosen = jnp.logical_and(slot_ids == slot, entry < act_count[column]).astype(settled.dtype)
            update = update + chosen[None, :, None, None, None] * tendency[:, None]
        return update

    updates = lax.map(one_column, jnp.arange(columns, dtype=jnp.int32))
    updates = jnp.transpose(updates, (1, 2, 3, 0, 4, 5)).reshape(NB, SLOTS, NZ, columns * BX, BY)
    return settled + time_step * updates
```

```python
import functools

import jax
import jax.numpy as jnp
from jax import lax
from jax.experimental import pallas as pl
from jax.experimental.pallas import tpu as pltpu
from jax.sharding import PartitionSpec as P

courant = 0.04
time_step = 2.0
f32 = jnp.float32
bf16 = jnp.bfloat16


def pieces(ref):
    return ref.reshape(ref.shape[0] * ref.shape[1] * ref.shape[2] * ref.shape[3], ref.shape[4])


def edges_body(spec_ref, head_ref, tail_ref):
    bins, _, nz, bx, _ = spec_ref.shape
    flat = pieces(spec_ref)

    def level(z, carry):
        for x in range(3):
            for first, out in ((0, head_ref), (bx - 3, tail_ref)):
                rows = flat[pl.ds(z * bx + first + x, bins, stride=nz * bx), :]
                out[0, z, x] = rows.astype(bf16)
        return carry

    lax.fori_loop(0, nz, level, 0)


def advect_cells(p, pos, half_cw, sixth_cw):
    u = [jnp.where(pos, p[k], p[13 - k]) for k in range(13)]
    d = [u[k + 1] - u[k] for k in range(12)]
    s, ss, first, left, mid, right = {}, {}, {}, {}, {}, {}
    for j in range(1, 12):
        s[j] = d[j] - d[j - 1]
        ss[j] = s[j] + s[j]
        t = d[j] + d[j - 1]
        h = s[j] * s[j] * (13.0 / 3.0) + 4e-6
        if j <= 9:
            first[j] = t + ss[j]
            b = h + first[j] * first[j]
            left[j] = b * b
        if 2 <= j <= 10:
            b = h + t * t
            mid[j] = b * b
        if j >= 3:
            t = t - ss[j]
            b = h + t * t
            right[j] = b * b
    r = []
    for g in range(9):
        a, b, c = left[g + 1], mid[g + 2], right[g + 3]
        wl = b * c
        a3 = a * 3.0
        wm = a3 * (c + c)
        wr = a3 * b
        num = wl * ss[g + 1] + wm * ss[g + 2] + wr * (ss[g + 2] + (s[g + 2] - s[g + 3]))
        r.append(num / (wl + wm + wr))
    moved = [u[m + 3] - (half_cw * first[m + 2] + sixth_cw * (r[m + 1] - r[m])) for m in range(8)]
    return [jnp.where(pos, moved[i], moved[7 - i]) for i in range(8)]


def transport_body(order_ref, spec_ref, left_ref, right_ref, wind_ref, fall_ref, out_ref, pick_ref):
    bins, _, nz, bx, by = spec_ref.shape
    flat, flat_out = pieces(spec_ref), pieces(out_ref)
    active = pl.program_id(0) < pl.num_programs(0) // 2

    for half in range(bins // 8):
        first = half * 8
        fall = fall_ref[first : first + 8, :]

        def level(step, above, first=first, fall=fall):
            z = nz - 1 - step
            speed = jnp.broadcast_to(wind_ref[0, pl.ds(z, 1), :], (8, by))
            pos = speed > 0
            cw = courant * jnp.abs(speed)
            own = [flat[pl.ds(first * nz * bx + z * bx + x, 8, stride=nz * bx), :] for x in range(bx)]
            head = [left_ref[0, z, x, first : first + 8, :].astype(f32) for x in range(3)]
            tail = [right_ref[0, z, x, first : first + 8, :].astype(f32) for x in range(3)]
            adv = advect_cells(head + own + tail, pos, cw * 0.5, cw * (1.0 / 6.0))
            settled = [adv[x] - fall * (adv[x] - above[x]) for x in range(bx)]
            for x in range(bx):
                flat_out[pl.ds(first * nz * bx + z * bx + x, 8, stride=nz * bx), :] = settled[x]

            @pl.when(active)
            def _():
                for x in range(bx):
                    pick_ref[0, z, x, first : first + 8, :] = settled[x].astype(bf16)

            return tuple(adv)

        lax.fori_loop(0, nz, level, tuple(jnp.zeros((8, by), f32) for _ in range(bx)))


def collect_body(got_ref, table_ref, out_ref, cells_ref, prod_ref):
    bx, by = got_ref.shape[3], got_ref.shape[5]

    def pair(step, carry):
        for part in range(2):
            x = step * 2 + part
            lanes = slice(part * by, (part + 1) * by)
            cells = [got_ref[q, 0, 0, x] for q in range(4)]
            for q in range(4):
                cells_ref[q * 16 : q * 16 + 16, :] = cells[q].astype(f32)
            row = 0
            for i in range(64):
                one = jnp.broadcast_to(cells_ref[i : i + 1, :], (16, by)).astype(bf16)
                for q in range(i // 16, 4):
                    prod_ref[row : row + 16, lanes] = one * cells[q]
                    row += 16
        total = jnp.dot(table_ref[...], prod_ref[...], preferred_element_type=f32).astype(bf16)
        for part in range(2):
            for q in range(4):
                out_ref[q, 0, 0, step * 2 + part] = total[q * 16 : q * 16 + 16, part * by : (part + 1) * by]
        return carry

    lax.fori_loop(0, bx // 2, pair, 0)


def update_body(order_ref, count_ref, settled_ref, tend_ref, out_ref):
    bins, _, nz, bx, by = settled_ref.shape
    flat, flat_out = pieces(settled_ref), pieces(out_ref)
    on = jnp.full((bins, by), pl.program_id(0), jnp.int32) < count_ref[0]

    def level(z, carry):
        for x in range(bx):
            where = pl.ds(z * bx + x, bins, stride=nz * bx)
            add = tend_ref[0, z, x].astype(f32) * time_step
            flat_out[where, :] = flat[where, :] + jnp.where(on, add, 0.0)
        return carry

    lax.fori_loop(0, nz, level, 0)


def pair_table(collection):
    t = jnp.transpose(collection, (2, 1, 0)).astype(f32)
    both = (t + jnp.transpose(t, (0, 2, 1))).astype(bf16)
    t = t.astype(bf16)
    parts = []
    for q in range(4):
        lo, hi = q * 16, q * 16 + 16
        rows = jnp.concatenate([t[:, lo:hi, lo:hi], both[:, lo:hi, hi:]], axis=2)
        parts.append(rows.reshape(64, -1))
    return jnp.concatenate(parts, axis=1)


def local(spectrum, wind, fall_speed, collection, act_order, act_count):
    bins, slots, nz, bx, by = spectrum.shape
    count = lax.axis_size("blk")
    order = act_order[0]
    half = slots // 2
    block = (bins, 1, nz, bx, by)
    side = (1, nz, 3, bins, by)
    side_shape = jax.ShapeDtypeStruct((slots, nz, 3, bins, by), bf16)

    heads, tails = pl.pallas_call(
        edges_body,
        grid=(slots,),
        in_specs=[pl.BlockSpec(block, lambda r: (0, r, 0, 0, 0))],
        out_specs=[pl.BlockSpec(side, lambda r: (r, 0, 0, 0, 0))] * 2,
        out_shape=[side_shape] * 2,
    )(spectrum)
    left = lax.ppermute(tails, "blk", [(i, i + 1) for i in range(count - 1)])
    right = lax.ppermute(heads, "blk", [(i + 1, i) for i in range(count - 1)])

    whole = lax.all_gather(collection, "bin", axis=2, tiled=True)
    table = pair_table(whole)

    fall = jnp.broadcast_to((courant * fall_speed)[:, None], (bins, by))
    settled, picked = pl.pallas_call(
        transport_body,
        grid_spec=pltpu.PrefetchScalarGridSpec(
            num_scalar_prefetch=1,
            grid=(slots,),
            in_specs=[
                pl.BlockSpec(block, lambda g, o: (0, o[g], 0, 0, 0)),
                pl.BlockSpec(side, lambda g, o: (o[g], 0, 0, 0, 0)),
                pl.BlockSpec(side, lambda g, o: (o[g], 0, 0, 0, 0)),
                pl.BlockSpec((1, nz, by), lambda g, o: (o[g], 0, 0)),
                pl.BlockSpec((bins, by), lambda g, o: (0, 0)),
            ],
            out_specs=[
                pl.BlockSpec(block, lambda g, o: (0, o[g], 0, 0, 0)),
                pl.BlockSpec((1, nz, bx, bins, by), lambda g, o: (jnp.minimum(g, 3), 0, 0, 0, 0)),
            ],
        ),
        out_shape=[
            jax.ShapeDtypeStruct(spectrum.shape, f32),
            jax.ShapeDtypeStruct((half, nz, bx, bins, by), bf16),
        ],
    )(order, spectrum, left, right, wind, fall)

    parts = 4
    share = nz // parts
    send = picked.reshape(half, parts, share, bx, bins, by)
    got = lax.all_to_all(jnp.moveaxis(send, 1, 0), "bin", 0, 0)
    tile = (parts, 1, 1, bx, bins, by)
    where = lambda a, z: (0, a, z, 0, 0, 0)
    tend = pl.pallas_call(
        collect_body,
        grid=(half, share),
        in_specs=[pl.BlockSpec(tile, where), pl.BlockSpec(table.shape, lambda a, z: (0, 0))],
        out_specs=pl.BlockSpec(tile, where),
        out_shape=jax.ShapeDtypeStruct((parts, half, share, bx, bins, by), bf16),
        scratch_shapes=[pltpu.VMEM((64, by), f32), pltpu.VMEM((2560, 2 * by), bf16)],
    )(got, table)
    back = lax.all_to_all(tend, "bin", 0, 0)
    back = jnp.moveaxis(back, 0, 1).reshape(half, nz, bx, bins, by)

    return pl.pallas_call(
        update_body,
        grid_spec=pltpu.PrefetchScalarGridSpec(
            num_scalar_prefetch=2,
            grid=(half,),
            in_specs=[
                pl.BlockSpec(block, lambda a, o, c: (0, o[a], 0, 0, 0)),
                pl.BlockSpec((1, nz, bx, bins, by), lambda a, o, c: (a, 0, 0, 0, 0)),
            ],
            out_specs=pl.BlockSpec(block, lambda a, o, c: (0, o[a], 0, 0, 0)),
        ),
        out_shape=jax.ShapeDtypeStruct(spectrum.shape, f32),
        input_output_aliases={2: 0},
    )(order, act_count, settled, back)


def solution(mesh):
    return jax.shard_map(
        local,
        mesh=mesh,
        in_specs=(
            P("bin", None, None, "blk", None),
            P(),
            P("bin"),
            P(None, None, "bin"),
            P("blk", None),
            P("blk"),
        ),
        out_specs=P("bin", None, None, "blk", None),
        check_vma=False,
    )
```

```python
import jax
import jax.numpy as jnp
from jax import lax
from jax.experimental import pallas as pl
from jax.experimental.pallas import tpu as pltpu
from jax.sharding import PartitionSpec as P

courant = 0.04
time_step = 2.0
f32 = jnp.float32
bf16 = jnp.bfloat16
MESH = pl.DeviceIdType.MESH


def pieces(ref):
    return ref.reshape(ref.shape[0] * ref.shape[1] * ref.shape[2] * ref.shape[3], ref.shape[4])


def advect_cells(p, pos, half_cw, sixth_cw):
    u = [jnp.where(pos, p[k], p[13 - k]) for k in range(13)]
    d = [u[k + 1] - u[k] for k in range(12)]
    s, ss, first, left, mid, right = {}, {}, {}, {}, {}, {}
    for j in range(1, 12):
        s[j] = d[j] - d[j - 1]
        ss[j] = s[j] + s[j]
        t = d[j] + d[j - 1]
        h = s[j] * s[j] * (13.0 / 3.0) + 4e-6
        if j <= 9:
            first[j] = t + ss[j]
            b = h + first[j] * first[j]
            left[j] = b * b
        if 2 <= j <= 10:
            b = h + t * t
            mid[j] = b * b
        if j >= 3:
            t = t - ss[j]
            b = h + t * t
            right[j] = b * b
    r = []
    for g in range(9):
        a, b, c = left[g + 1], mid[g + 2], right[g + 3]
        wl = b * c
        a3 = a * 3.0
        wm = a3 * (c + c)
        wr = a3 * b
        num = wl * ss[g + 1] + wm * ss[g + 2] + wr * (ss[g + 2] + (s[g + 2] - s[g + 3]))
        r.append(num / (wl + wm + wr))
    moved = [u[m + 3] - (half_cw * first[m + 2] + sixth_cw * (r[m + 1] - r[m])) for m in range(8)]
    return [jnp.where(pos, moved[i], moved[7 - i]) for i in range(8)]


def step_body(
    order_ref, left_order_ref, right_order_ref, spec_ref, wind_ref, fall_ref, own_table_ref,
    settled_out, back_out,
    table_ref, heads, tails, from_left, from_right, settled_ref, picks, got, tends, cells_ref, prod_ref,
    halo_sent, halo_got, pick_sent, pick_got, back_sent, back_got, table_sent, table_got, out_sem, own_sem,
):
    bins, slots, nz, bx, by = spec_ref.shape
    half = slots // 2
    flat = pieces(spec_ref)
    blk, bin_ = lax.axis_index("blk"), lax.axis_index("bin")
    n_blk, n_bin = lax.axis_size("blk"), lax.axis_size("bin")
    share = nz // n_bin
    last = n_blk - 1
    right, left = lax.rem(blk + 1, n_blk), lax.rem(blk + last, n_blk)
    peers = [lax.rem(bin_ + k, n_bin) for k in range(1, n_bin)]

    barrier = pltpu.get_barrier_semaphore()
    for side in (left, right):
        pl.semaphore_signal(barrier, inc=1, device_id={"blk": side}, device_id_type=MESH)
    for peer in peers:
        pl.semaphore_signal(barrier, inc=1, device_id={"bin": peer}, device_id_type=MESH)
    pl.semaphore_wait(barrier, 2 + n_bin - 1)

    def halos(g):
        return [
            pltpu.make_async_remote_copy(
                src.at[g], dst.at[g], halo_sent.at[k, g], halo_got.at[k, g], device_id={"blk": side}, device_id_type=MESH
            )
            for k, (src, dst, side) in enumerate(((tails, from_left, right), (heads, from_right, left)))
        ]

    def table_copies():
        mine = table_ref.at[pl.ds(pl.multiple_of(bin_ * bins, bins), bins)]
        return [
            pltpu.make_async_remote_copy(
                own_table_ref, mine, table_sent.at[k], table_got.at[k], device_id={"bin": peer}, device_id_type=MESH
            )
            for k, peer in enumerate(peers)
        ]

    def pick_copies(g):
        return [
            pltpu.make_async_remote_copy(
                picks.at[g, pl.ds(peer * share, share)], got.at[bin_, g], pick_sent.at[k, g], pick_got.at[k, g],
                device_id={"bin": peer}, device_id_type=MESH,
            )
            for k, peer in enumerate(peers)
        ]

    def back_copies(g):
        return [
            pltpu.make_async_remote_copy(
                tends.at[peer, g], back_out.at[g, pl.ds(bin_ * share, share)], back_sent.at[k, g], back_got.at[k, g],
                device_id={"bin": peer}, device_id_type=MESH,
            )
            for k, peer in enumerate(peers)
        ]

    def own_back(g):
        return pltpu.make_async_copy(tends.at[bin_, g], back_out.at[g, pl.ds(bin_ * share, share)], own_sem.at[g])

    def out_copy(g):
        return pltpu.make_async_copy(settled_ref.at[g], settled_out.at[g], out_sem.at[g])

    def pack(g):
        to_left, to_right = left_order_ref[g] * nz * bx, right_order_ref[g] * nz * bx

        def level(z, carry):
            for x in range(3):
                rows = flat[pl.ds(to_left + z * bx + x, bins, stride=slots * nz * bx), :]
                heads[g, z, x] = rows.astype(bf16)
                rows = flat[pl.ds(to_right + z * bx + bx - 3 + x, bins, stride=slots * nz * bx), :]
                tails[g, z, x] = rows.astype(bf16)
            return carry

        lax.fori_loop(0, nz, level, 0)

    def pack_and_send(g, carry):
        pack(g)
        for copy in halos(g):
            copy.start()
        return carry

    lax.fori_loop(0, half, pack_and_send, 0)
    for copy in table_copies():
        copy.start()
    table_ref[pl.ds(pl.multiple_of(bin_ * bins, bins), bins), :] = own_table_ref[...]

    def pack_later(g, carry):
        pack(g)
        return carry

    lax.fori_loop(half, slots, pack_later, 0)

    def transport(g):
        row = order_ref[g]
        for first in range(0, bins, 8):
            fall = fall_ref[first : first + 8, :]
            start = (first * slots + row) * nz * bx

            def level(step, above, first=first, fall=fall, start=start):
                z = nz - 1 - step
                speed = jnp.broadcast_to(wind_ref[row, pl.ds(z, 1), :], (8, by))
                pos = speed > 0
                cw = courant * jnp.abs(speed)
                own = [flat[pl.ds(start + z * bx + x, 8, stride=slots * nz * bx), :] for x in range(bx)]
                head = [from_left[g, z, x, first : first + 8, :].astype(f32) for x in range(3)]
                tail = [from_right[g, z, x, first : first + 8, :].astype(f32) for x in range(3)]
                adv = advect_cells(head + own + tail, pos, cw * 0.5, cw * (1.0 / 6.0))
                for x in range(bx):
                    settled_ref[g, z, x, first : first + 8, :] = adv[x] - fall * (adv[x] - above[x])
                return tuple(adv)

            lax.fori_loop(0, nz, level, tuple(jnp.zeros((8, by), f32) for _ in range(bx)))

    def pick(g):
        def level(z, carry):
            for x in range(bx):
                picks[g, z, x] = settled_ref[g, z, x].astype(bf16)
            return carry

        lax.fori_loop(0, nz, level, 0)

    def collect(g):
        def pair(step, carry):
            zz, first = step // (bx // 2), step % (bx // 2) * 2
            for part in range(2):
                lanes = slice(part * by, (part + 1) * by)
                cells = [got[q, g, zz, first + part] for q in range(n_bin)]
                for q in range(n_bin):
                    cells_ref[q * bins : q * bins + bins, :] = cells[q].astype(f32)
                row = 0
                for i in range(n_bin * bins):
                    one = jnp.broadcast_to(cells_ref[i : i + 1, :], (bins, by)).astype(bf16)
                    for q in range(i // bins, n_bin):
                        prod_ref[row : row + bins, lanes] = one * cells[q]
                        row += bins
            total = jnp.dot(table_ref[...], prod_ref[...], preferred_element_type=f32).astype(bf16)
            for part in range(2):
                for q in range(n_bin):
                    tends[q, g, zz, first + part] = total[q * bins : q * bins + bins, part * by : (part + 1) * by]
            return carry

        lax.fori_loop(0, share * bx // 2, pair, 0)

    def slot(g, carry):
        for copy in halos(g):
            copy.wait_recv()

        @pl.when(blk == 0)
        def _():
            from_left[g] = jnp.zeros(from_left.shape[1:], bf16)

        @pl.when(blk == last)
        def _():
            from_right[g] = jnp.zeros(from_right.shape[1:], bf16)

        transport(g)
        out_copy(g).start()

        @pl.when(g < half)
        def _():
            pick(g)
            for copy in pick_copies(g):
                copy.start()
            got[bin_, g] = picks[g, pl.ds(bin_ * share, share)]
            for copy in halos(g + half):
                copy.start()

        @pl.when(g == 1)
        def _():
            for copy in table_copies():
                copy.wait_recv()

        @pl.when(jnp.logical_and(g >= 1, g <= half))
        def _():
            for copy in pick_copies(g - 1):
                copy.wait_recv()
            collect(g - 1)
            for copy in back_copies(g - 1):
                copy.start()
            own_back(g - 1).start()

        return carry

    lax.fori_loop(0, slots, slot, 0)

    for copy in table_copies():
        copy.wait_send()

    def finish(g, carry):
        for copy in halos(g):
            copy.wait_send()
        out_copy(g).wait()
        return carry

    lax.fori_loop(0, slots, finish, 0)

    def finish_active(g, carry):
        for copy in pick_copies(g):
            copy.wait_send()
        for copy in back_copies(g):
            copy.wait()
        own_back(g).wait()
        return carry

    lax.fori_loop(0, half, finish_active, 0)


def update_body(order_ref, count_ref, settled_ref, tend_ref, out_ref):
    bins, _, nz, bx, by = out_ref.shape
    flat_out = pieces(out_ref)
    on = jnp.full((bins, by), pl.program_id(0), jnp.int32) < count_ref[0]

    def level(z, carry):
        for x in range(bx):
            add = tend_ref[0, z, x].astype(f32) * time_step
            flat_out[pl.ds(z * bx + x, bins, stride=nz * bx), :] = settled_ref[0, z, x] + jnp.where(on, add, 0.0)
        return carry

    lax.fori_loop(0, nz, level, 0)


def pair_table(collection):
    t = jnp.transpose(collection, (2, 1, 0)).astype(f32)
    both = (t + jnp.transpose(t, (0, 2, 1))).astype(bf16)
    t = t.astype(bf16)
    parts = []
    for q in range(4):
        lo, hi = q * 16, q * 16 + 16
        rows = jnp.concatenate([t[:, lo:hi, lo:hi], both[:, lo:hi, hi:]], axis=2)
        parts.append(rows.reshape(t.shape[0], -1))
    return jnp.concatenate(parts, axis=1)


def local(spectrum, wind, fall_speed, collection, act_order, act_count):
    bins, slots, nz, bx, by = spectrum.shape
    n_blk, n_bin = lax.axis_size("blk"), lax.axis_size("bin")
    half, share, every = slots // 2, nz // n_bin, bins * n_bin
    order = act_order[0]
    left_order = lax.ppermute(order, "blk", [(i, (i + 1) % n_blk) for i in range(n_blk)])
    right_order = lax.ppermute(order, "blk", [((i + 1) % n_blk, i) for i in range(n_blk)])
    table = pair_table(collection)
    fall = jnp.broadcast_to((courant * fall_speed)[:, None], (bins, by))

    smem, vmem, hbm = (pl.BlockSpec(memory_space=s) for s in (pltpu.SMEM, pltpu.VMEM, pl.ANY))
    side = pltpu.VMEM((slots, nz, 3, bins, by), bf16)
    dma = pltpu.SemaphoreType.DMA
    settled, back = pl.pallas_call(
        step_body,
        in_specs=[smem] * 3 + [vmem] * 4,
        out_specs=[hbm] * 2,
        out_shape=[
            jax.ShapeDtypeStruct((slots, nz, bx, bins, by), f32),
            jax.ShapeDtypeStruct((half, nz, bx, bins, by), bf16),
        ],
        scratch_shapes=[
            pltpu.VMEM((every, table.shape[1]), bf16),
            side, side, side, side,
            pltpu.VMEM((slots, nz, bx, bins, by), f32),
            pltpu.VMEM((half, nz, bx, bins, by), bf16),
            pltpu.VMEM((n_bin, half, share, bx, bins, by), bf16),
            pltpu.VMEM((n_bin, half, share, bx, bins, by), bf16),
            pltpu.VMEM((every, by), f32),
            pltpu.VMEM((table.shape[1], 2 * by), bf16),
            dma((2, slots)), dma((2, slots)),
            dma((n_bin - 1, half)), dma((n_bin - 1, half)),
            dma((n_bin - 1, half)), dma((n_bin - 1, half)),
            dma((n_bin - 1,)), dma((n_bin - 1,)),
            dma((slots,)), dma((half,)),
        ],
        compiler_params=pltpu.CompilerParams(collective_id=0, has_side_effects=True, vmem_limit_bytes=48 << 20),
    )(order, left_order, right_order, spectrum, wind, fall, table)

    return pl.pallas_call(
        update_body,
        grid_spec=pltpu.PrefetchScalarGridSpec(
            num_scalar_prefetch=2,
            grid=(slots,),
            in_specs=[
                pl.BlockSpec((1, nz, bx, bins, by), lambda g, o, c: (g, 0, 0, 0, 0)),
                pl.BlockSpec((1, nz, bx, bins, by), lambda g, o, c: (jnp.minimum(g, half - 1), 0, 0, 0, 0)),
            ],
            out_specs=pl.BlockSpec((bins, 1, nz, bx, by), lambda g, o, c: (0, o[g], 0, 0, 0)),
        ),
        out_shape=jax.ShapeDtypeStruct(spectrum.shape, f32),
    )(order, act_count, settled, back)


def solution(mesh):
    return jax.shard_map(
        local,
        mesh=mesh,
        in_specs=(
            P("bin", None, None, "blk", None),
            P(),
            P("bin"),
            P(None, None, "bin"),
            P("blk", None),
            P("blk"),
        ),
        out_specs=P("bin", None, None, "blk", None),
        check_vma=False,
    )
```

```python
import jax
import jax.numpy as jnp
from jax import lax
from jax.experimental import pallas as pl
from jax.experimental.pallas import tpu as pltpu
from jax.sharding import PartitionSpec as P

courant = 0.04
time_step = 2.0
f32 = jnp.float32
bf16 = jnp.bfloat16
MESH = pl.DeviceIdType.MESH


def pieces(ref):
    return ref.reshape(ref.shape[0] * ref.shape[1] * ref.shape[2] * ref.shape[3], ref.shape[4])


def advect_cells(p, pos, half_cw, sixth_cw):
    u = [jnp.where(pos, p[k], p[13 - k]) for k in range(13)]
    d = [u[k + 1] - u[k] for k in range(12)]
    s, ss, first, left, mid, right = {}, {}, {}, {}, {}, {}
    for j in range(1, 12):
        s[j] = d[j] - d[j - 1]
        ss[j] = s[j] + s[j]
        t = d[j] + d[j - 1]
        h = s[j] * s[j] * (13.0 / 3.0) + 4e-6
        if j <= 9:
            first[j] = t + ss[j]
            b = h + first[j] * first[j]
            left[j] = b * b
        if 2 <= j <= 10:
            b = h + t * t
            mid[j] = b * b
        if j >= 3:
            t = t - ss[j]
            b = h + t * t
            right[j] = b * b
    r = []
    for g in range(9):
        a, b, c = left[g + 1], mid[g + 2], right[g + 3]
        wl = b * c
        a3 = a * 3.0
        wm = a3 * (c + c)
        wr = a3 * b
        num = wl * ss[g + 1] + wm * ss[g + 2] + wr * (ss[g + 2] + (s[g + 2] - s[g + 3]))
        r.append(num / (wl + wm + wr))
    moved = [u[m + 3] - (half_cw * first[m + 2] + sixth_cw * (r[m + 1] - r[m])) for m in range(8)]
    return [jnp.where(pos, moved[i], moved[7 - i]) for i in range(8)]


def step_body(
    order_rows, fall_speed_ref, spec_hbm, wind_ref, own_table_ref,
    settled_ref, back_out,
    spec_ref, rows_got, orders, own_order, fall_ref,
    table_ref, heads, tails, from_left, from_right, picks, got, tends, cells_ref, prod_ref,
    thirds, third_left, third_on, third_right, third_sent, third_got, on_sent, on_got,
    halo_sent, halo_got, pick_sent, pick_got, back_sent, back_got, table_sent, table_got, own_sem,
    spec_sem, rows_sent, rows_recv, orders_sem, own_order_sem,
):
    bins, slots, nz, bx, by = spec_hbm.shape
    half = slots // 2
    flat = pieces(spec_ref)
    spec_copies = [pltpu.make_async_copy(spec_hbm.at[b], spec_ref.at[b], spec_sem.at[b]) for b in range(bins)]
    for copy in spec_copies:
        copy.start()
    blk, bin_ = lax.axis_index("blk"), lax.axis_index("bin")
    n_blk, n_bin = lax.axis_size("blk"), lax.axis_size("bin")
    share = nz // n_bin
    last = n_blk - 1
    right, left = lax.rem(blk + 1, n_blk), lax.rem(blk + last, n_blk)
    right2, left2 = lax.rem(blk + 2, n_blk), lax.rem(blk + last - 1, n_blk)
    sibling, across = bin_ + 1 - 2 * lax.rem(bin_, 2), lax.rem(bin_ + 2, n_bin)
    peers = [lax.rem(bin_ + k, n_bin) for k in range(1, n_bin)]

    barrier = pltpu.get_barrier_semaphore()
    for side in (left, right, left2, right2):
        pl.semaphore_signal(barrier, inc=1, device_id={"blk": side}, device_id_type=MESH)
    for peer in peers:
        pl.semaphore_signal(barrier, inc=1, device_id={"bin": peer}, device_id_type=MESH)
    pl.semaphore_wait(barrier, 4 + n_bin - 1)

    row_copies = [
        pltpu.make_async_remote_copy(
            order_rows, rows_got.at[k], rows_sent.at[k], rows_recv.at[k], device_id={"blk": side}, device_id_type=MESH
        )
        for k, side in enumerate((right, left, right2))
    ]
    for copy in row_copies:
        copy.start()
    for b in range(bins):
        fall_ref[b : b + 1, :] = jnp.full((1, by), fall_speed_ref[b], f32) * courant

    def halos(g):
        return [
            pltpu.make_async_remote_copy(
                src.at[g], dst.at[g], halo_sent.at[k, g], halo_got.at[k, g], device_id={"blk": side}, device_id_type=MESH
            )
            for k, (src, dst, side) in enumerate(((tails, from_left, right), (heads, from_right, left)))
        ]

    def table_part(q):
        return table_ref.at[pl.ds(pl.multiple_of(q * bins, bins), bins)]

    def table_copy(k):
        src, part, peer = (
            (own_table_ref, table_part(bin_), sibling),
            (own_table_ref, table_part(bin_), across),
            (table_part(across), table_part(across), sibling),
        )[k]
        return pltpu.make_async_remote_copy(
            src, part, table_sent.at[k], table_got.at[k], device_id={"bin": peer}, device_id_type=MESH
        )

    def third_copy(r):
        return pltpu.make_async_remote_copy(
            thirds.at[r], third_left.at[r], third_sent.at[r], third_got.at[r], device_id={"blk": right}, device_id_type=MESH
        )

    def on_copy(g):
        return pltpu.make_async_remote_copy(
            third_on.at[g], third_right.at[g], on_sent.at[g], on_got.at[g], device_id={"blk": left2}, device_id_type=MESH
        )

    def pick_copies(g):
        return [
            pltpu.make_async_remote_copy(
                picks.at[g, pl.ds(peer * share, share)], got.at[bin_, g], pick_sent.at[k, g], pick_got.at[k, g],
                device_id={"bin": peer}, device_id_type=MESH,
            )
            for k, peer in enumerate(peers)
        ]

    def back_copies(g):
        return [
            pltpu.make_async_remote_copy(
                tends.at[peer, g], back_out.at[g, pl.ds(bin_ * share, share)], back_sent.at[k, g], back_got.at[k, g],
                device_id={"bin": peer}, device_id_type=MESH,
            )
            for k, peer in enumerate(peers)
        ]

    def own_back(g):
        return pltpu.make_async_copy(tends.at[bin_, g], back_out.at[g, pl.ds(bin_ * share, share)], own_sem.at[g])

    def pack(g):
        to_left, to_right = orders[0, g, 0] * nz * bx, orders[1, g, 0] * nz * bx

        def level(z, carry):
            for x in range(2):
                rows = flat[pl.ds(to_left + z * bx + x, bins, stride=slots * nz * bx), :]
                heads[g, z, x] = rows.astype(bf16)
                rows = flat[pl.ds(to_right + z * bx + bx - 2 + x, bins, stride=slots * nz * bx), :]
                tails[g, z, x] = rows.astype(bf16)
            return carry

        lax.fori_loop(0, nz, level, 0)

    def pack_third(r, carry):
        def level(z, inner):
            low = flat[pl.ds(r * nz * bx + z * bx + 2, bins, stride=slots * nz * bx), :]
            high = flat[pl.ds(r * nz * bx + z * bx + bx - 3, bins, stride=slots * nz * bx), :]
            pos = jnp.broadcast_to(wind_ref[z, pl.ds(r, 1), :], (bins, by)) > 0
            thirds[r, z] = jnp.where(pos, high, low).astype(bf16)
            return inner

        lax.fori_loop(0, nz, level, 0)
        third_copy(r).start()
        return carry

    def pass_on(g, carry):
        row = orders[2, g, 0]
        for z in range(nz):
            third_on[g, z] = third_left[row, z]
        on_copy(g).start()
        return carry

    def pack_and_send(g, carry):
        pack(g)
        for copy in halos(g):
            copy.start()
        return carry

    own_order_copy = pltpu.make_async_copy(order_rows, own_order, own_order_sem)
    own_order_copy.start()
    for copy in spec_copies:
        copy.wait()
    lax.fori_loop(0, slots, pack_third, 0)
    for copy in row_copies:
        copy.wait_recv()
    orders_copy = pltpu.make_async_copy(rows_got, orders, orders_sem)
    orders_copy.start()
    orders_copy.wait()
    own_order_copy.wait()
    lax.fori_loop(0, half, pack_and_send, 0)
    table_copy(0).start()
    table_copy(1).start()
    table_ref[pl.ds(pl.multiple_of(bin_ * bins, bins), bins), :] = own_table_ref[...]

    def pack_later(g, carry):
        pack(g)
        return carry

    lax.fori_loop(half, slots, pack_later, 0)

    def third_arrived(r, carry):
        third_copy(r).wait_recv()
        return carry

    lax.fori_loop(0, slots, third_arrived, 0)
    lax.fori_loop(0, slots, pass_on, 0)

    @pl.when(blk == 0)
    def _():
        third_left[...] = jnp.zeros(third_left.shape, bf16)

    def transport(g):
        row = own_order[g, 0]
        for first in range(0, bins, 8):
            fall = fall_ref[first : first + 8, :]
            start = (first * slots + row) * nz * bx

            def level(step, above, first=first, fall=fall, start=start):
                z = nz - 1 - step
                speed = jnp.broadcast_to(wind_ref[z, pl.ds(row, 1), :], (8, by))
                pos = speed > 0
                cw = courant * jnp.abs(speed)
                own = [flat[pl.ds(start + z * bx + x, 8, stride=slots * nz * bx), :] for x in range(bx)]
                head = [from_left[g, z, x, first : first + 8, :].astype(f32) for x in range(2)]
                tail = [from_right[g, z, x, first : first + 8, :].astype(f32) for x in range(2)]
                head = [third_left[row, z, first : first + 8, :].astype(f32)] + head
                tail = tail + [third_right[g, z, first : first + 8, :].astype(f32)]
                adv = advect_cells(head + own + tail, pos, cw * 0.5, cw * (1.0 / 6.0))
                for x in range(bx):
                    settled_ref[g, z, x, first : first + 8, :] = adv[x] - fall * (adv[x] - above[x])
                return tuple(adv)

            lax.fori_loop(0, nz, level, tuple(jnp.zeros((8, by), f32) for _ in range(bx)))

    def pick(g):
        def level(z, carry):
            for x in range(bx):
                picks[g, z, x] = settled_ref[g, z, x].astype(bf16)
            return carry

        lax.fori_loop(0, nz, level, 0)

    def collect(g):
        def pair(step, carry):
            zz, first = step // (bx // 2), step % (bx // 2) * 2
            for part in range(2):
                lanes = slice(part * by, (part + 1) * by)
                cells = [got[q, g, zz, first + part] for q in range(n_bin)]
                for q in range(n_bin):
                    cells_ref[q * bins : q * bins + bins, :] = cells[q].astype(f32)
                row = 0
                for i in range(n_bin * bins):
                    one = jnp.broadcast_to(cells_ref[i : i + 1, :], (bins, by)).astype(bf16)
                    for q in range(i // bins, n_bin):
                        prod_ref[row : row + bins, lanes] = one * cells[q]
                        row += bins
            total = jnp.dot(table_ref[...], prod_ref[...], preferred_element_type=f32).astype(bf16)
            for part in range(2):
                for q in range(n_bin):
                    tends[q, g, zz, first + part] = total[q * bins : q * bins + bins, part * by : (part + 1) * by]
            return carry

        lax.fori_loop(0, share * bx // 2, pair, 0)

    def slot(g, carry):
        on_copy(g).wait_recv()
        for copy in halos(g):
            copy.wait_recv()

        @pl.when(blk == 0)
        def _():
            from_left[g] = jnp.zeros(from_left.shape[1:], bf16)

        @pl.when(blk == last)
        def _():
            from_right[g] = jnp.zeros(from_right.shape[1:], bf16)
            third_right[g] = jnp.zeros(third_right.shape[1:], bf16)

        transport(g)

        @pl.when(g < half)
        def _():
            pick(g)
            for copy in pick_copies(g):
                copy.start()
            got[bin_, g] = picks[g, pl.ds(bin_ * share, share)]
            for copy in halos(g + half):
                copy.start()

        @pl.when(g == 0)
        def _():
            table_copy(1).wait_recv()
            table_copy(2).start()

        @pl.when(g == 1)
        def _():
            table_copy(0).wait_recv()
            table_copy(2).wait_recv()

        @pl.when(jnp.logical_and(g >= 1, g <= half))
        def _():
            for copy in pick_copies(g - 1):
                copy.wait_recv()
            collect(g - 1)
            for copy in back_copies(g - 1):
                copy.start()
            own_back(g - 1).start()

        return carry

    lax.fori_loop(0, slots, slot, 0)

    for copy in row_copies + [table_copy(k) for k in range(3)]:
        copy.wait_send()

    def finish(g, carry):
        third_copy(g).wait_send()
        on_copy(g).wait_send()
        for copy in halos(g):
            copy.wait_send()
        return carry

    lax.fori_loop(0, slots, finish, 0)

    def finish_active(g, carry):
        for copy in pick_copies(g):
            copy.wait_send()
        for copy in back_copies(g):
            copy.wait()
        own_back(g).wait()
        return carry

    lax.fori_loop(0, half, finish_active, 0)


def update_body(order_ref, count_ref, settled_ref, tend_ref, out_ref, rows_ref, out_sem):
    bins, slots, nz, bx, by = out_ref.shape
    half = slots // 2

    def copy(g):
        return pltpu.make_async_copy(rows_ref.at[g], out_ref.at[:, order_ref[g]], out_sem.at[g])

    def active(g, carry):
        on = jnp.full((bx, bins, by), g, jnp.int32) < count_ref[0]

        def level(z, inner):
            add = tend_ref[g, z].astype(f32) * time_step
            rows_ref[g, :, z] = jnp.swapaxes(settled_ref[g, z] + jnp.where(on, add, 0.0), 0, 1)
            return inner

        lax.fori_loop(0, nz, level, 0)
        copy(g).start()
        return carry

    def idle(g, carry):
        def level(z, inner):
            rows_ref[g, :, z] = jnp.swapaxes(settled_ref[g, z], 0, 1)
            return inner

        lax.fori_loop(0, nz, level, 0)
        copy(g).start()
        return carry

    lax.fori_loop(0, half, active, 0)
    lax.fori_loop(half, slots, idle, 0)

    def finish(g, carry):
        copy(g).wait()
        return carry

    lax.fori_loop(0, slots, finish, 0)


def pair_table(collection):
    t = jnp.transpose(collection, (2, 1, 0)).astype(f32)
    both = (t + jnp.transpose(t, (0, 2, 1))).astype(bf16)
    t = t.astype(bf16)
    parts = []
    for q in range(4):
        lo, hi = q * 16, q * 16 + 16
        rows = jnp.concatenate([t[:, lo:hi, lo:hi], both[:, lo:hi, hi:]], axis=2)
        parts.append(rows.reshape(t.shape[0], -1))
    return jnp.concatenate(parts, axis=1)


def local(spectrum, wind, fall_speed, collection, act_order, act_count):
    bins, slots, nz, bx, by = spectrum.shape
    n_blk, n_bin = lax.axis_size("blk"), lax.axis_size("bin")
    half, share, every = slots // 2, nz // n_bin, bins * n_bin
    order = act_order[0]
    order_rows = jnp.broadcast_to(order[:, None], (slots, by))
    table = pair_table(collection)

    smem, vmem, hbm = (pl.BlockSpec(memory_space=s) for s in (pltpu.SMEM, pltpu.VMEM, pl.ANY))
    side = pltpu.VMEM((slots, nz, 2, bins, by), bf16)
    third = pltpu.VMEM((slots, nz, bins, by), bf16)
    dma = pltpu.SemaphoreType.DMA
    settled, back = pl.pallas_call(
        step_body,
        in_specs=[vmem, smem, pl.BlockSpec(memory_space=pltpu.HBM), vmem, vmem],
        out_specs=[vmem, hbm],
        out_shape=[
            jax.ShapeDtypeStruct((slots, nz, bx, bins, by), f32),
            jax.ShapeDtypeStruct((half, nz, bx, bins, by), bf16),
        ],
        scratch_shapes=[
            pltpu.VMEM(spectrum.shape, f32),
            pltpu.VMEM((3, slots, by), jnp.int32),
            pltpu.SMEM((3, slots, by), jnp.int32),
            pltpu.SMEM((slots, by), jnp.int32),
            pltpu.VMEM((bins, by), f32),
            pltpu.VMEM((every, table.shape[1]), bf16),
            side, side, side, side,
            pltpu.VMEM((half, nz, bx, bins, by), bf16),
            pltpu.VMEM((n_bin, half, share, bx, bins, by), bf16),
            pltpu.VMEM((n_bin, half, share, bx, bins, by), bf16),
            pltpu.VMEM((every, by), f32),
            pltpu.VMEM((table.shape[1], 2 * by), bf16),
            third, third, third, third,
            dma((slots,)), dma((slots,)), dma((slots,)), dma((slots,)),
            dma((2, slots)), dma((2, slots)),
            dma((n_bin - 1, half)), dma((n_bin - 1, half)),
            dma((n_bin - 1, half)), dma((n_bin - 1, half)),
            dma((n_bin - 1,)), dma((n_bin - 1,)),
            dma((half,)), dma((bins,)), dma((3,)), dma((3,)), dma(()), dma(()),
        ],
        compiler_params=pltpu.CompilerParams(collective_id=0, has_side_effects=True, vmem_limit_bytes=42 << 20),
    )(order_rows, fall_speed, spectrum, jnp.transpose(wind, (1, 0, 2)), table)

    return pl.pallas_call(
        update_body,
        in_specs=[smem, smem, vmem, vmem],
        out_specs=hbm,
        out_shape=jax.ShapeDtypeStruct(spectrum.shape, f32),
        scratch_shapes=[pltpu.VMEM((slots, bins, nz, bx, by), f32), dma((slots,))],
        compiler_params=pltpu.CompilerParams(vmem_limit_bytes=16 << 20),
    )(order, act_count, settled, back)


def solution(mesh):
    return jax.shard_map(
        local,
        mesh=mesh,
        in_specs=(
            P("bin", None, None, "blk", None),
            P(),
            P("bin"),
            P(None, None, "bin"),
            P("blk", None),
            P("blk"),
        ),
        out_specs=P("bin", None, None, "blk", None),
        check_vma=False,
    )
```

```python
import jax
import jax.numpy as jnp
from jax import lax
from jax.experimental import pallas as pl
from jax.experimental.pallas import tpu as pltpu
from jax.sharding import PartitionSpec as P

courant = 0.04
time_step = 2.0
f32 = jnp.float32
bf16 = jnp.bfloat16
MESH = pl.DeviceIdType.MESH


def pieces(ref):
    return ref.reshape(ref.shape[0] * ref.shape[1] * ref.shape[2] * ref.shape[3], ref.shape[4])


def advect_cells(p, pos, half_cw, sixth_cw):
    u = [jnp.where(pos, p[k], p[13 - k]) for k in range(13)]
    d = [u[k + 1] - u[k] for k in range(12)]
    s, ss, first, left, mid, right = {}, {}, {}, {}, {}, {}
    for j in range(1, 12):
        s[j] = d[j] - d[j - 1]
        ss[j] = s[j] + s[j]
        t = d[j] + d[j - 1]
        h = s[j] * s[j] * (13.0 / 3.0) + 4e-6
        if j <= 9:
            first[j] = t + ss[j]
            b = h + first[j] * first[j]
            left[j] = b * b
        if 2 <= j <= 10:
            b = h + t * t
            mid[j] = b * b
        if j >= 3:
            t = t - ss[j]
            b = h + t * t
            right[j] = b * b
    r = []
    for g in range(9):
        a, b, c = left[g + 1], mid[g + 2], right[g + 3]
        wl = b * c
        a3 = a * 3.0
        wm = a3 * (c + c)
        wr = a3 * b
        num = wl * ss[g + 1] + wm * ss[g + 2] + wr * (ss[g + 2] + (s[g + 2] - s[g + 3]))
        r.append(num / (wl + wm + wr))
    moved = [u[m + 3] - (half_cw * first[m + 2] + sixth_cw * (r[m + 1] - r[m])) for m in range(8)]
    return [jnp.where(pos, moved[i], moved[7 - i]) for i in range(8)]


def pair_table(coll_ref, by_bin, sums, table_ref):
    every, bins, _ = coll_ref.shape
    by_bin[...] = jnp.swapaxes(coll_ref[...].astype(f32), 0, 1)

    def one_bin(k, carry):
        both = by_bin[k]
        by_bin[k] = both + both.T
        return carry

    lax.fori_loop(0, bins, one_bin, 0)
    sums[...] = jnp.swapaxes(by_bin[...], 0, 1)
    lane = lax.broadcasted_iota(jnp.int32, (bins, every), 1)
    column = 0
    for first in range(0, every, bins):
        own_group = lane < first + bins
        parts = []
        for i in range(first, first + bins):
            parts.append(jnp.where(own_group, coll_ref[i].astype(f32), sums[i])[:, first:])
        block = jnp.concatenate(parts, axis=1).astype(bf16)
        table_ref[:, column : column + block.shape[1]] = block
        column += block.shape[1]


def step_body(
    order_hbm, fall_hbm, spec_hbm, wind_hbm, coll_hbm,
    settled_ref, back_out,
    spec_ref, wind_ref, coll_ref, own_table_ref, by_bin, sums, order_rows, fall_speed_ref,
    rows_got, orders, own_order, fall_ref,
    table_ref, heads, tails, from_left, from_right, picks, got, tends, cells_ref, prod_ref,
    thirds, third_left, third_on, third_right, third_sent, third_got, on_sent, on_got,
    halo_sent, halo_got, pick_sent, pick_got, back_sent, back_got, table_sent, table_got, own_sem,
    spec_sem, small_sem, rows_sent, rows_recv, orders_sem,
):
    bins, slots, nz, bx, by = spec_hbm.shape
    half = slots // 2
    flat = pieces(spec_ref)
    small_copies = [
        pltpu.make_async_copy(src, dst, small_sem.at[k])
        for k, (src, dst) in enumerate(
            ((order_hbm, order_rows), (order_hbm, own_order), (fall_hbm, fall_speed_ref), (wind_hbm, wind_ref), (coll_hbm, coll_ref))
        )
    ]
    for copy in small_copies[:4]:
        copy.start()

    def spec_copy(r):
        return pltpu.make_async_copy(spec_hbm.at[:, r], spec_ref.at[:, r], spec_sem.at[r])

    for r in range(slots):
        spec_copy(r).start()
    small_copies[4].start()
    blk, bin_ = lax.axis_index("blk"), lax.axis_index("bin")
    n_blk, n_bin = lax.axis_size("blk"), lax.axis_size("bin")
    share = nz // n_bin
    last = n_blk - 1
    right, left = lax.rem(blk + 1, n_blk), lax.rem(blk + last, n_blk)
    right2, left2 = lax.rem(blk + 2, n_blk), lax.rem(blk + last - 1, n_blk)
    sibling, across = bin_ + 1 - 2 * lax.rem(bin_, 2), lax.rem(bin_ + 2, n_bin)
    peers = [lax.rem(bin_ + k, n_bin) for k in range(1, n_bin)]

    barrier = pltpu.get_barrier_semaphore()
    for side in (left, right, left2, right2):
        pl.semaphore_signal(barrier, inc=1, device_id={"blk": side}, device_id_type=MESH)
    for peer in peers:
        pl.semaphore_signal(barrier, inc=1, device_id={"bin": peer}, device_id_type=MESH)
    pl.semaphore_wait(barrier, 4 + n_bin - 1)

    row_copies = [
        pltpu.make_async_remote_copy(
            order_rows, rows_got.at[k], rows_sent.at[k], rows_recv.at[k], device_id={"blk": side}, device_id_type=MESH
        )
        for k, side in enumerate((right, left, right2))
    ]
    small_copies[0].wait()
    for copy in row_copies:
        copy.start()
    for copy in small_copies[1:4]:
        copy.wait()

    def halos(g):
        return [
            pltpu.make_async_remote_copy(
                src.at[g], dst.at[g], halo_sent.at[k, g], halo_got.at[k, g], device_id={"blk": side}, device_id_type=MESH
            )
            for k, (src, dst, side) in enumerate(((tails, from_left, right), (heads, from_right, left)))
        ]

    def table_part(q):
        return table_ref.at[pl.ds(pl.multiple_of(q * bins, bins), bins)]

    def table_copy(k):
        src, part, peer = (
            (own_table_ref, table_part(bin_), sibling),
            (own_table_ref, table_part(bin_), across),
            (table_part(across), table_part(across), sibling),
        )[k]
        return pltpu.make_async_remote_copy(
            src, part, table_sent.at[k], table_got.at[k], device_id={"bin": peer}, device_id_type=MESH
        )

    def third_copy(r):
        return pltpu.make_async_remote_copy(
            thirds.at[r], third_left.at[r], third_sent.at[r], third_got.at[r], device_id={"blk": right}, device_id_type=MESH
        )

    def on_copy(g):
        return pltpu.make_async_remote_copy(
            third_on.at[g], third_right.at[g], on_sent.at[g], on_got.at[g], device_id={"blk": left2}, device_id_type=MESH
        )

    def pick_copies(g):
        return [
            pltpu.make_async_remote_copy(
                picks.at[g, pl.ds(peer * share, share)], got.at[bin_, g], pick_sent.at[k, g], pick_got.at[k, g],
                device_id={"bin": peer}, device_id_type=MESH,
            )
            for k, peer in enumerate(peers)
        ]

    def back_copies(g):
        return [
            pltpu.make_async_remote_copy(
                tends.at[peer, g], back_out.at[g, pl.ds(bin_ * share, share)], back_sent.at[k, g], back_got.at[k, g],
                device_id={"bin": peer}, device_id_type=MESH,
            )
            for k, peer in enumerate(peers)
        ]

    def own_back(g):
        return pltpu.make_async_copy(tends.at[bin_, g], back_out.at[g, pl.ds(bin_ * share, share)], own_sem.at[g])

    def pack(g):
        to_left, to_right = orders[0, 0, g] * nz * bx, orders[1, 0, g] * nz * bx

        def level(z, carry):
            for x in range(2):
                rows = flat[pl.ds(to_left + z * bx + x, bins, stride=slots * nz * bx), :]
                heads[g, z, x] = rows.astype(bf16)
                rows = flat[pl.ds(to_right + z * bx + bx - 2 + x, bins, stride=slots * nz * bx), :]
                tails[g, z, x] = rows.astype(bf16)
            return carry

        lax.fori_loop(0, nz, level, 0)

    def pack_third(r, carry):
        spec_copy(r).wait()

        def level(z, inner):
            low = flat[pl.ds(r * nz * bx + z * bx + 2, bins, stride=slots * nz * bx), :]
            high = flat[pl.ds(r * nz * bx + z * bx + bx - 3, bins, stride=slots * nz * bx), :]
            pos = jnp.broadcast_to(wind_ref[z, pl.ds(r, 1), :], (bins, by)) > 0
            thirds[r, z] = jnp.where(pos, high, low).astype(bf16)
            return inner

        lax.fori_loop(0, nz, level, 0)
        third_copy(r).start()
        return carry

    def pass_on(g, carry):
        row = orders[2, 0, g]
        for z in range(nz):
            third_on[g, z] = third_left[row, z]
        on_copy(g).start()
        return carry

    def pack_and_send(g, carry):
        pack(g)
        for copy in halos(g):
            copy.start()
        return carry

    lax.fori_loop(0, slots, pack_third, 0)
    for copy in row_copies:
        copy.wait_recv()
    orders_copy = pltpu.make_async_copy(rows_got, orders, orders_sem)
    orders_copy.start()
    orders_copy.wait()
    lax.fori_loop(0, half, pack_and_send, 0)
    for b in range(bins):
        fall_ref[b : b + 1, :] = jnp.full((1, by), fall_speed_ref[b], f32) * courant
    small_copies[4].wait()
    pair_table(coll_ref, by_bin, sums, own_table_ref)
    table_copy(0).start()
    table_copy(1).start()
    table_ref[pl.ds(pl.multiple_of(bin_ * bins, bins), bins), :] = own_table_ref[...]

    def pack_later(g, carry):
        pack(g)
        return carry

    lax.fori_loop(half, slots, pack_later, 0)

    def third_arrived(r, carry):
        third_copy(r).wait_recv()
        return carry

    lax.fori_loop(0, slots, third_arrived, 0)
    lax.fori_loop(0, slots, pass_on, 0)

    @pl.when(blk == 0)
    def _():
        third_left[...] = jnp.zeros(third_left.shape, bf16)

    def transport(g):
        row = own_order[0, g]
        for first in range(0, bins, 8):
            fall = fall_ref[first : first + 8, :]
            start = (first * slots + row) * nz * bx

            def level(step, above, first=first, fall=fall, start=start):
                z = nz - 1 - step
                speed = jnp.broadcast_to(wind_ref[z, pl.ds(row, 1), :], (8, by))
                pos = speed > 0
                cw = courant * jnp.abs(speed)
                own = [flat[pl.ds(start + z * bx + x, 8, stride=slots * nz * bx), :] for x in range(bx)]
                head = [from_left[g, z, x, first : first + 8, :].astype(f32) for x in range(2)]
                tail = [from_right[g, z, x, first : first + 8, :].astype(f32) for x in range(2)]
                head = [third_left[row, z, first : first + 8, :].astype(f32)] + head
                tail = tail + [third_right[g, z, first : first + 8, :].astype(f32)]
                adv = advect_cells(head + own + tail, pos, cw * 0.5, cw * (1.0 / 6.0))
                for x in range(bx):
                    settled_ref[g, z, x, first : first + 8, :] = adv[x] - fall * (adv[x] - above[x])
                return tuple(adv)

            lax.fori_loop(0, nz, level, tuple(jnp.zeros((8, by), f32) for _ in range(bx)))

    def pick(g):
        def level(z, carry):
            for x in range(bx):
                picks[g, z, x] = settled_ref[g, z, x].astype(bf16)
            return carry

        lax.fori_loop(0, nz, level, 0)

    def collect(g):
        def pair(step, carry):
            zz, first = step // (bx // 2), step % (bx // 2) * 2
            for part in range(2):
                lanes = slice(part * by, (part + 1) * by)
                cells = [got[q, g, zz, first + part] for q in range(n_bin)]
                for q in range(n_bin):
                    cells_ref[q * bins : q * bins + bins, :] = cells[q].astype(f32)
                row = 0
                for i in range(n_bin * bins):
                    one = jnp.broadcast_to(cells_ref[i : i + 1, :], (bins, by)).astype(bf16)
                    for q in range(i // bins, n_bin):
                        prod_ref[row : row + bins, lanes] = one * cells[q]
                        row += bins
            total = jnp.dot(table_ref[...], prod_ref[...], preferred_element_type=f32).astype(bf16)
            for part in range(2):
                for q in range(n_bin):
                    tends[q, g, zz, first + part] = total[q * bins : q * bins + bins, part * by : (part + 1) * by]
            return carry

        lax.fori_loop(0, share * bx // 2, pair, 0)

    def slot(g, carry):
        on_copy(g).wait_recv()
        for copy in halos(g):
            copy.wait_recv()

        @pl.when(blk == 0)
        def _():
            from_left[g] = jnp.zeros(from_left.shape[1:], bf16)

        @pl.when(blk == last)
        def _():
            from_right[g] = jnp.zeros(from_right.shape[1:], bf16)
            third_right[g] = jnp.zeros(third_right.shape[1:], bf16)

        transport(g)

        @pl.when(g < half)
        def _():
            pick(g)
            for copy in pick_copies(g):
                copy.start()
            got[bin_, g] = picks[g, pl.ds(bin_ * share, share)]
            for copy in halos(g + half):
                copy.start()

        @pl.when(g == 0)
        def _():
            table_copy(1).wait_recv()
            table_copy(2).start()

        @pl.when(g == 1)
        def _():
            table_copy(0).wait_recv()
            table_copy(2).wait_recv()

        @pl.when(jnp.logical_and(g >= 1, g <= half))
        def _():
            for copy in pick_copies(g - 1):
                copy.wait_recv()
            collect(g - 1)
            for copy in back_copies(g - 1):
                copy.start()
            own_back(g - 1).start()

        return carry

    lax.fori_loop(0, slots, slot, 0)

    for copy in row_copies + [table_copy(k) for k in range(3)]:
        copy.wait_send()

    def finish(g, carry):
        third_copy(g).wait_send()
        on_copy(g).wait_send()
        for copy in halos(g):
            copy.wait_send()
        return carry

    lax.fori_loop(0, slots, finish, 0)

    def finish_active(g, carry):
        for copy in pick_copies(g):
            copy.wait_send()
        for copy in back_copies(g):
            copy.wait()
        own_back(g).wait()
        return carry

    lax.fori_loop(0, half, finish_active, 0)


def update_body(order_ref, count_ref, settled_ref, tend_ref, out_ref, rows_ref, out_sem):
    bins, slots, nz, bx, by = out_ref.shape
    half = slots // 2

    def copy(g):
        return pltpu.make_async_copy(rows_ref.at[g], out_ref.at[:, order_ref[g]], out_sem.at[g])

    def active(g, carry):
        on = jnp.full((bx, bins, by), g, jnp.int32) < count_ref[0]

        def level(z, inner):
            add = tend_ref[g, z].astype(f32) * time_step
            rows_ref[g, :, z] = jnp.swapaxes(settled_ref[g, z] + jnp.where(on, add, 0.0), 0, 1)
            return inner

        lax.fori_loop(0, nz, level, 0)
        copy(g).start()
        return carry

    def idle(g, carry):
        def level(z, inner):
            rows_ref[g, :, z] = jnp.swapaxes(settled_ref[g, z], 0, 1)
            return inner

        lax.fori_loop(0, nz, level, 0)
        copy(g).start()
        return carry

    lax.fori_loop(0, half, active, 0)
    lax.fori_loop(half, slots, idle, 0)

    def finish(g, carry):
        copy(g).wait()
        return carry

    lax.fori_loop(0, slots, finish, 0)


def local(spectrum, wind, fall_speed, collection, act_order, act_count):
    bins, slots, nz, bx, by = spectrum.shape
    n_blk, n_bin = lax.axis_size("blk"), lax.axis_size("bin")
    half, share, every = slots // 2, nz // n_bin, bins * n_bin
    order = act_order[0]
    pairs = sum(bins * (every - first) for first in range(0, every, bins))

    inputs = (act_order, fall_speed, spectrum, jnp.transpose(wind, (1, 0, 2)), jnp.transpose(collection, (0, 2, 1)))

    smem, vmem, hbm = (pl.BlockSpec(memory_space=s) for s in (pltpu.SMEM, pltpu.VMEM, pl.ANY))
    side = pltpu.VMEM((slots, nz, 2, bins, by), bf16)
    third = pltpu.VMEM((slots, nz, bins, by), bf16)
    dma = pltpu.SemaphoreType.DMA
    settled, back = pl.pallas_call(
        step_body,
        in_specs=[pl.BlockSpec(memory_space=pltpu.HBM)] * 5,
        out_specs=[vmem, hbm],
        out_shape=[
            jax.ShapeDtypeStruct((slots, nz, bx, bins, by), f32),
            jax.ShapeDtypeStruct((half, nz, bx, bins, by), bf16),
        ],
        scratch_shapes=[
            pltpu.VMEM(spectrum.shape, f32),
            pltpu.VMEM((nz, slots, by), f32),
            pltpu.VMEM((every, bins, every), bf16),
            pltpu.VMEM((bins, pairs), bf16),
            pltpu.VMEM((bins, every, every), f32),
            pltpu.VMEM((every, bins, every), f32),
            pltpu.VMEM((1, slots), jnp.int32),
            pltpu.SMEM((bins,), f32),
            pltpu.VMEM((3, 1, slots), jnp.int32),
            pltpu.SMEM((3, 1, slots), jnp.int32),
            pltpu.SMEM((1, slots), jnp.int32),
            pltpu.VMEM((bins, by), f32),
            pltpu.VMEM((every, pairs), bf16),
            side, side, side, side,
            pltpu.VMEM((half, nz, bx, bins, by), bf16),
            pltpu.VMEM((n_bin, half, share, bx, bins, by), bf16),
            pltpu.VMEM((n_bin, half, share, bx, bins, by), bf16),
            pltpu.VMEM((every, by), f32),
            pltpu.VMEM((pairs, 2 * by), bf16),
            third, third, third, third,
            dma((slots,)), dma((slots,)), dma((slots,)), dma((slots,)),
            dma((2, slots)), dma((2, slots)),
            dma((n_bin - 1, half)), dma((n_bin - 1, half)),
            dma((n_bin - 1, half)), dma((n_bin - 1, half)),
            dma((n_bin - 1,)), dma((n_bin - 1,)),
            dma((half,)), dma((slots,)), dma((5,)), dma((3,)), dma((3,)), dma(()),
        ],
        compiler_params=pltpu.CompilerParams(collective_id=0, has_side_effects=True, vmem_limit_bytes=42 << 20),
    )(*(pltpu.with_memory_space_constraint(a, pltpu.HBM) for a in inputs))

    return pl.pallas_call(
        update_body,
        in_specs=[smem, smem, vmem, vmem],
        out_specs=hbm,
        out_shape=jax.ShapeDtypeStruct(spectrum.shape, f32),
        scratch_shapes=[pltpu.VMEM((slots, bins, nz, bx, by), f32), dma((slots,))],
        compiler_params=pltpu.CompilerParams(vmem_limit_bytes=16 << 20),
    )(order, act_count, settled, back)


def solution(mesh):
    return jax.shard_map(
        local,
        mesh=mesh,
        in_specs=(
            P("bin", None, None, "blk", None),
            P(),
            P("bin"),
            P(None, None, "bin"),
            P("blk", None),
            P("blk"),
        ),
        out_specs=P("bin", None, None, "blk", None),
        check_vma=False,
    )
```

```python
import jax
import jax.numpy as jnp
from jax import lax
from jax.experimental import pallas as pl
from jax.experimental.pallas import tpu as pltpu
from jax.sharding import PartitionSpec as P

courant = 0.04
time_step = 2.0
f32 = jnp.float32
bf16 = jnp.bfloat16
MESH = pl.DeviceIdType.MESH


def pieces(ref):
    return ref.reshape(ref.shape[0] * ref.shape[1] * ref.shape[2] * ref.shape[3], ref.shape[4])


def advect_cells(p, pos, half_cw, sixth_cw):
    u = [jnp.where(pos, p[k], p[13 - k]) for k in range(13)]
    d = [u[k + 1] - u[k] for k in range(12)]
    s, ss, first, left, mid, right = {}, {}, {}, {}, {}, {}
    for j in range(1, 12):
        s[j] = d[j] - d[j - 1]
        ss[j] = s[j] + s[j]
        t = d[j] + d[j - 1]
        h = s[j] * s[j] * (13.0 / 3.0) + 4e-6
        if j <= 9:
            first[j] = t + ss[j]
            b = h + first[j] * first[j]
            left[j] = b * b
        if 2 <= j <= 10:
            b = h + t * t
            mid[j] = b * b
        if j >= 3:
            t = t - ss[j]
            b = h + t * t
            right[j] = b * b
    r = []
    for g in range(9):
        a, b, c = left[g + 1], mid[g + 2], right[g + 3]
        wl = b * c
        a3 = a * 3.0
        wm = a3 * (c + c)
        wr = a3 * b
        num = wl * ss[g + 1] + wm * ss[g + 2] + wr * (ss[g + 2] + (s[g + 2] - s[g + 3]))
        r.append(num / (wl + wm + wr))
    moved = [u[m + 3] - (half_cw * first[m + 2] + sixth_cw * (r[m + 1] - r[m])) for m in range(8)]
    return [jnp.where(pos, moved[i], moved[7 - i]) for i in range(8)]


def pair_table(coll_ref, by_bin, sums, table_ref):
    every, bins, _ = coll_ref.shape
    by_bin[...] = jnp.swapaxes(coll_ref[...].astype(f32), 0, 1)

    def one_bin(k, carry):
        both = by_bin[k]
        by_bin[k] = both + both.T
        return carry

    lax.fori_loop(0, bins, one_bin, 0)
    sums[...] = jnp.swapaxes(by_bin[...], 0, 1)
    lane = lax.broadcasted_iota(jnp.int32, (bins, every), 1)
    column = 0
    for first in range(0, every, bins):
        own_group = lane < first + bins
        parts = []
        for i in range(first, first + bins):
            parts.append(jnp.where(own_group, coll_ref[i].astype(f32), sums[i])[:, first:])
        block = jnp.concatenate(parts, axis=1).astype(bf16)
        table_ref[:, column : column + block.shape[1]] = block
        column += block.shape[1]


def step_body(
    order_hbm, fall_hbm, spec_hbm, wind_hbm, coll_hbm,
    settled_ref, back_out,
    spec_ref, wind_ref, coll_ref, own_table_ref, by_bin, sums, order_rows, fall_speed_ref,
    rows_got, orders, own_order, fall_ref,
    table_ref, heads, tails, from_left, from_right, picks, got, tends, cells_ref, prod_ref,
    thirds, third_left, third_on, third_right, third_sent, third_got, on_sent, on_got,
    halo_sent, halo_got, pick_sent, pick_got, back_sent, back_got, table_sent, table_got, own_sem,
    spec_sem, small_sem, rows_sent, rows_recv, orders_sem,
):
    bins, slots, nz, bx, by = spec_hbm.shape
    half = slots // 2
    flat = pieces(spec_ref)
    small_copies = [
        pltpu.make_async_copy(src, dst, small_sem.at[k])
        for k, (src, dst) in enumerate(
            ((order_hbm, order_rows), (order_hbm, own_order), (fall_hbm, fall_speed_ref), (wind_hbm, wind_ref), (coll_hbm, coll_ref))
        )
    ]
    for copy in small_copies[:4]:
        copy.start()

    def spec_copy(r):
        return pltpu.make_async_copy(spec_hbm.at[:, r], spec_ref.at[:, r], spec_sem.at[r])

    for r in range(slots):
        spec_copy(r).start()
    small_copies[4].start()
    blk, bin_ = lax.axis_index("blk"), lax.axis_index("bin")
    n_blk, n_bin = lax.axis_size("blk"), lax.axis_size("bin")
    share = nz // n_bin
    last = n_blk - 1
    right, left = lax.rem(blk + 1, n_blk), lax.rem(blk + last, n_blk)
    right2, left2 = lax.rem(blk + 2, n_blk), lax.rem(blk + last - 1, n_blk)
    sibling, across = bin_ + 1 - 2 * lax.rem(bin_, 2), lax.rem(bin_ + 2, n_bin)
    pair = blk + 1 - 2 * lax.rem(blk, 2)
    peers = [lax.rem(bin_ + k, n_bin) for k in range(1, n_bin)]

    barrier = pltpu.get_barrier_semaphore()
    for side in (left, right, left2, right2):
        pl.semaphore_signal(barrier, inc=1, device_id={"blk": side}, device_id_type=MESH)
    for peer in peers:
        pl.semaphore_signal(barrier, inc=1, device_id={"bin": peer}, device_id_type=MESH)
    pl.semaphore_signal(barrier, inc=1, device_id={"blk": pair, "bin": across}, device_id_type=MESH)
    pl.semaphore_wait(barrier, 5 + n_bin - 1)

    row_copies = [
        pltpu.make_async_remote_copy(
            order_rows, rows_got.at[k], rows_sent.at[k], rows_recv.at[k], device_id={"blk": side}, device_id_type=MESH
        )
        for k, side in enumerate((right, left, right2))
    ]
    small_copies[0].wait()
    for copy in row_copies:
        copy.start()
    for copy in small_copies[1:4]:
        copy.wait()

    def halos(g):
        return [
            pltpu.make_async_remote_copy(
                src.at[g], dst.at[g], halo_sent.at[k, g], halo_got.at[k, g], device_id={"blk": side}, device_id_type=MESH
            )
            for k, (src, dst, side) in enumerate(((tails, from_left, right), (heads, from_right, left)))
        ]

    def table_part(q):
        return table_ref.at[pl.ds(pl.multiple_of(q * bins, bins), bins)]

    def table_copy(k):
        src, part, peer = (
            (own_table_ref, table_part(bin_), {"bin": sibling}),
            (own_table_ref, table_part(bin_), {"blk": pair, "bin": across}),
            (table_part(across), table_part(across), {"bin": sibling}),
        )[k]
        return pltpu.make_async_remote_copy(
            src, part, table_sent.at[k], table_got.at[k], device_id=peer, device_id_type=MESH
        )

    def third_copy(r):
        return pltpu.make_async_remote_copy(
            thirds.at[r], third_left.at[r], third_sent.at[r], third_got.at[r], device_id={"blk": right}, device_id_type=MESH
        )

    def on_copy(g):
        return pltpu.make_async_remote_copy(
            third_on.at[g], third_right.at[g], on_sent.at[g], on_got.at[g], device_id={"blk": left2}, device_id_type=MESH
        )

    def pick_copies(g):
        return [
            pltpu.make_async_remote_copy(
                picks.at[g, pl.ds(peer * share, share)], got.at[bin_, g], pick_sent.at[k, g], pick_got.at[k, g],
                device_id={"bin": peer}, device_id_type=MESH,
            )
            for k, peer in enumerate(peers)
        ]

    def back_copies(g):
        return [
            pltpu.make_async_remote_copy(
                tends.at[peer, g], back_out.at[g, pl.ds(bin_ * share, share)], back_sent.at[k, g], back_got.at[k, g],
                device_id={"bin": peer}, device_id_type=MESH,
            )
            for k, peer in enumerate(peers)
        ]

    def own_back(g):
        return pltpu.make_async_copy(tends.at[bin_, g], back_out.at[g, pl.ds(bin_ * share, share)], own_sem.at[g])

    def pack(g):
        to_left, to_right = orders[0, 0, g] * nz * bx, orders[1, 0, g] * nz * bx

        def level(z, carry):
            for x in range(2):
                rows = flat[pl.ds(to_left + z * bx + x, bins, stride=slots * nz * bx), :]
                heads[g, z, x] = rows.astype(bf16)
                rows = flat[pl.ds(to_right + z * bx + bx - 2 + x, bins, stride=slots * nz * bx), :]
                tails[g, z, x] = rows.astype(bf16)
            return carry

        lax.fori_loop(0, nz, level, 0)

    def pack_third(r, carry):
        spec_copy(r).wait()

        def level(z, inner):
            low = flat[pl.ds(r * nz * bx + z * bx + 2, bins, stride=slots * nz * bx), :]
            high = flat[pl.ds(r * nz * bx + z * bx + bx - 3, bins, stride=slots * nz * bx), :]
            pos = jnp.broadcast_to(wind_ref[z, pl.ds(r, 1), :], (bins, by)) > 0
            thirds[r, z] = jnp.where(pos, high, low).astype(bf16)
            return inner

        lax.fori_loop(0, nz, level, 0)
        third_copy(r).start()
        return carry

    def pass_on(g, carry):
        row = orders[2, 0, g]
        for z in range(nz):
            third_on[g, z] = third_left[row, z]
        on_copy(g).start()
        return carry

    def pack_and_send(g, carry):
        pack(g)
        for copy in halos(g):
            copy.start()
        return carry

    lax.fori_loop(0, slots, pack_third, 0)
    for copy in row_copies:
        copy.wait_recv()
    orders_copy = pltpu.make_async_copy(rows_got, orders, orders_sem)
    orders_copy.start()
    orders_copy.wait()
    lax.fori_loop(0, half, pack_and_send, 0)
    for b in range(bins):
        fall_ref[b : b + 1, :] = jnp.full((1, by), fall_speed_ref[b], f32) * courant
    small_copies[4].wait()
    pair_table(coll_ref, by_bin, sums, own_table_ref)
    table_copy(0).start()
    table_copy(1).start()
    table_ref[pl.ds(pl.multiple_of(bin_ * bins, bins), bins), :] = own_table_ref[...]

    def pack_later(g, carry):
        pack(g)
        return carry

    lax.fori_loop(half, slots, pack_later, 0)

    def third_arrived(r, carry):
        third_copy(r).wait_recv()
        return carry

    lax.fori_loop(0, slots, third_arrived, 0)
    lax.fori_loop(0, slots, pass_on, 0)

    @pl.when(blk == 0)
    def _():
        third_left[...] = jnp.zeros(third_left.shape, bf16)

    def transport(g):
        row = own_order[0, g]
        for first in range(0, bins, 8):
            fall = fall_ref[first : first + 8, :]
            start = (first * slots + row) * nz * bx

            def level(step, above, first=first, fall=fall, start=start):
                z = nz - 1 - step
                speed = jnp.broadcast_to(wind_ref[z, pl.ds(row, 1), :], (8, by))
                pos = speed > 0
                cw = courant * jnp.abs(speed)
                own = [flat[pl.ds(start + z * bx + x, 8, stride=slots * nz * bx), :] for x in range(bx)]
                head = [from_left[g, z, x, first : first + 8, :].astype(f32) for x in range(2)]
                tail = [from_right[g, z, x, first : first + 8, :].astype(f32) for x in range(2)]
                head = [third_left[row, z, first : first + 8, :].astype(f32)] + head
                tail = tail + [third_right[g, z, first : first + 8, :].astype(f32)]
                adv = advect_cells(head + own + tail, pos, cw * 0.5, cw * (1.0 / 6.0))
                settled = jnp.stack([adv[x] - fall * (adv[x] - above[x]) for x in range(bx)])
                settled_ref[g, first : first + 8, z] = jnp.swapaxes(settled, 0, 1)

                @pl.when(g < half)
                def _():
                    for x in range(bx):
                        picks[g, z, x, first : first + 8, :] = settled[x].astype(bf16)

                return tuple(adv)

            lax.fori_loop(0, nz, level, tuple(jnp.zeros((8, by), f32) for _ in range(bx)))

    def collect(g):
        def pair(step, carry):
            zz, first = step // (bx // 2), step % (bx // 2) * 2
            for part in range(2):
                lanes = slice(part * by, (part + 1) * by)
                cells = [got[q, g, zz, first + part] for q in range(n_bin)]
                for q in range(n_bin):
                    cells_ref[q * bins : q * bins + bins, :] = cells[q].astype(f32)
                row = 0
                for i in range(n_bin * bins):
                    one = jnp.broadcast_to(cells_ref[i : i + 1, :], (bins, by)).astype(bf16)
                    for q in range(i // bins, n_bin):
                        prod_ref[row : row + bins, lanes] = one * cells[q]
                        row += bins
            total = jnp.dot(table_ref[...], prod_ref[...], preferred_element_type=f32).astype(bf16)
            for part in range(2):
                for q in range(n_bin):
                    tends[q, g, zz, first + part] = total[q * bins : q * bins + bins, part * by : (part + 1) * by]
            return carry

        lax.fori_loop(0, share * bx // 2, pair, 0)

    def slot(g, carry):
        on_copy(g).wait_recv()
        for copy in halos(g):
            copy.wait_recv()

        @pl.when(blk == 0)
        def _():
            from_left[g] = jnp.zeros(from_left.shape[1:], bf16)

        @pl.when(blk == last)
        def _():
            from_right[g] = jnp.zeros(from_right.shape[1:], bf16)
            third_right[g] = jnp.zeros(third_right.shape[1:], bf16)

        transport(g)

        @pl.when(g < half)
        def _():
            for copy in pick_copies(g):
                copy.start()
            got[bin_, g] = picks[g, pl.ds(bin_ * share, share)]
            for copy in halos(g + half):
                copy.start()

        @pl.when(g == 0)
        def _():
            table_copy(1).wait_recv()
            table_copy(2).start()

        @pl.when(g == 1)
        def _():
            table_copy(0).wait_recv()
            table_copy(2).wait_recv()

        @pl.when(jnp.logical_and(g >= 1, g <= half))
        def _():
            for copy in pick_copies(g - 1):
                copy.wait_recv()
            collect(g - 1)
            for copy in back_copies(g - 1):
                copy.start()
            own_back(g - 1).start()

        return carry

    lax.fori_loop(0, slots, slot, 0)

    for copy in row_copies + [table_copy(k) for k in range(3)]:
        copy.wait_send()

    def finish(g, carry):
        third_copy(g).wait_send()
        on_copy(g).wait_send()
        for copy in halos(g):
            copy.wait_send()
        return carry

    lax.fori_loop(0, slots, finish, 0)

    def finish_active(g, carry):
        for copy in pick_copies(g):
            copy.wait_send()
        for copy in back_copies(g):
            copy.wait()
        own_back(g).wait()
        return carry

    lax.fori_loop(0, half, finish_active, 0)


def update_body(order_ref, count_ref, settled_ref, tend_ref, out_ref, rows_ref, out_sem):
    slots = settled_ref.shape[0]
    half, bins, nz, bx, by = rows_ref.shape

    def copy(src, g):
        return pltpu.make_async_copy(src.at[g], out_ref.at[:, order_ref[g]], out_sem.at[g])

    for g in range(half, slots):
        copy(settled_ref, g).start()

    def active(g, carry):
        on = jnp.full((bins, bx, by), g, jnp.int32) < count_ref[0]

        def level(z, inner):
            add = jnp.swapaxes(tend_ref[g, z].astype(f32), 0, 1) * time_step
            rows_ref[g, :, z] = settled_ref[g, :, z] + jnp.where(on, add, 0.0)
            return inner

        lax.fori_loop(0, nz, level, 0)
        copy(rows_ref, g).start()
        return carry

    lax.fori_loop(0, half, active, 0)
    for g in range(half):
        copy(rows_ref, g).wait()
    for g in range(half, slots):
        copy(settled_ref, g).wait()


def local(spectrum, wind, fall_speed, collection, act_order, act_count):
    bins, slots, nz, bx, by = spectrum.shape
    n_blk, n_bin = lax.axis_size("blk"), lax.axis_size("bin")
    half, share, every = slots // 2, nz // n_bin, bins * n_bin
    order = act_order[0]
    pairs = sum(bins * (every - first) for first in range(0, every, bins))

    inputs = (act_order, fall_speed, spectrum, jnp.transpose(wind, (1, 0, 2)), jnp.transpose(collection, (0, 2, 1)))

    smem, vmem, hbm = (pl.BlockSpec(memory_space=s) for s in (pltpu.SMEM, pltpu.VMEM, pl.ANY))
    side = pltpu.VMEM((slots, nz, 2, bins, by), bf16)
    third = pltpu.VMEM((slots, nz, bins, by), bf16)
    dma = pltpu.SemaphoreType.DMA
    settled, back = pl.pallas_call(
        step_body,
        in_specs=[pl.BlockSpec(memory_space=pltpu.HBM)] * 5,
        out_specs=[vmem, hbm],
        out_shape=[
            jax.ShapeDtypeStruct((slots, bins, nz, bx, by), f32),
            jax.ShapeDtypeStruct((half, nz, bx, bins, by), bf16),
        ],
        scratch_shapes=[
            pltpu.VMEM(spectrum.shape, f32),
            pltpu.VMEM((nz, slots, by), f32),
            pltpu.VMEM((every, bins, every), bf16),
            pltpu.VMEM((bins, pairs), bf16),
            pltpu.VMEM((bins, every, every), f32),
            pltpu.VMEM((every, bins, every), f32),
            pltpu.VMEM((1, slots), jnp.int32),
            pltpu.SMEM((bins,), f32),
            pltpu.VMEM((3, 1, slots), jnp.int32),
            pltpu.SMEM((3, 1, slots), jnp.int32),
            pltpu.SMEM((1, slots), jnp.int32),
            pltpu.VMEM((bins, by), f32),
            pltpu.VMEM((every, pairs), bf16),
            side, side, side, side,
            pltpu.VMEM((half, nz, bx, bins, by), bf16),
            pltpu.VMEM((n_bin, half, share, bx, bins, by), bf16),
            pltpu.VMEM((n_bin, half, share, bx, bins, by), bf16),
            pltpu.VMEM((every, by), f32),
            pltpu.VMEM((pairs, 2 * by), bf16),
            third, third, third, third,
            dma((slots,)), dma((slots,)), dma((slots,)), dma((slots,)),
            dma((2, slots)), dma((2, slots)),
            dma((n_bin - 1, half)), dma((n_bin - 1, half)),
            dma((n_bin - 1, half)), dma((n_bin - 1, half)),
            dma((n_bin - 1,)), dma((n_bin - 1,)),
            dma((half,)), dma((slots,)), dma((5,)), dma((3,)), dma((3,)), dma(()),
        ],
        compiler_params=pltpu.CompilerParams(collective_id=0, has_side_effects=True, vmem_limit_bytes=42 << 20),
    )(*(pltpu.with_memory_space_constraint(a, pltpu.HBM) for a in inputs))

    return pl.pallas_call(
        update_body,
        in_specs=[smem, smem, vmem, vmem],
        out_specs=hbm,
        out_shape=jax.ShapeDtypeStruct(spectrum.shape, f32),
        scratch_shapes=[pltpu.VMEM((half, bins, nz, bx, by), f32), dma((slots,))],
        compiler_params=pltpu.CompilerParams(vmem_limit_bytes=16 << 20),
    )(order, act_count, settled, back)


def solution(mesh):
    return jax.shard_map(
        local,
        mesh=mesh,
        in_specs=(
            P("bin", None, None, "blk", None),
            P(),
            P("bin"),
            P(None, None, "bin"),
            P("blk", None),
            P("blk"),
        ),
        out_specs=P("bin", None, None, "blk", None),
        check_vma=False,
    )
```

```python
import jax
import jax.numpy as jnp
from jax import lax
from jax.experimental import pallas as pl
from jax.experimental.pallas import tpu as pltpu
from jax.sharding import PartitionSpec as P

courant = 0.04
time_step = 2.0
f32 = jnp.float32
bf16 = jnp.bfloat16
MESH = pl.DeviceIdType.MESH


def pieces(ref):
    return ref.reshape(ref.shape[0] * ref.shape[1] * ref.shape[2] * ref.shape[3], ref.shape[4])


def advect_cells(p, pos, half_cw, sixth_cw):
    u = [jnp.where(pos, p[k], p[13 - k]) for k in range(13)]
    d = [u[k + 1] - u[k] for k in range(12)]
    s, ss, first, left, mid, right = {}, {}, {}, {}, {}, {}
    for j in range(1, 12):
        s[j] = d[j] - d[j - 1]
        ss[j] = s[j] + s[j]
        t = d[j] + d[j - 1]
        h = s[j] * s[j] * (13.0 / 3.0) + 4e-6
        if j <= 9:
            first[j] = t + ss[j]
            b = h + first[j] * first[j]
            left[j] = b * b
        if 2 <= j <= 10:
            b = h + t * t
            mid[j] = b * b
        if j >= 3:
            t = t - ss[j]
            b = h + t * t
            right[j] = b * b
    r = []
    for g in range(9):
        a, b, c = left[g + 1], mid[g + 2], right[g + 3]
        wl = b * c
        a3 = a * 3.0
        wm = a3 * (c + c)
        wr = a3 * b
        num = wl * ss[g + 1] + wm * ss[g + 2] + wr * (ss[g + 2] + (s[g + 2] - s[g + 3]))
        r.append(num / (wl + wm + wr))
    moved = [u[m + 3] - (half_cw * first[m + 2] + sixth_cw * (r[m + 1] - r[m])) for m in range(8)]
    return [jnp.where(pos, moved[i], moved[7 - i]) for i in range(8)]


def pair_table(coll_ref, by_bin, sums, table_ref):
    every, bins, _ = coll_ref.shape
    by_bin[...] = jnp.swapaxes(coll_ref[...].astype(f32), 0, 1)

    def one_bin(k, carry):
        both = by_bin[k]
        by_bin[k] = both + both.T
        return carry

    lax.fori_loop(0, bins, one_bin, 0)
    sums[...] = jnp.swapaxes(by_bin[...], 0, 1)
    lane = lax.broadcasted_iota(jnp.int32, (bins, every), 1)
    column = 0
    for first in range(0, every, bins):
        own_group = lane < first + bins
        parts = []
        for i in range(first, first + bins):
            parts.append(jnp.where(own_group, coll_ref[i].astype(f32), sums[i])[:, first:])
        block = jnp.concatenate(parts, axis=1).astype(bf16)
        table_ref[:, column : column + block.shape[1]] = block
        column += block.shape[1]


def step_body(
    order_hbm, fall_hbm, spec_hbm, wind_hbm, coll_hbm,
    settled_ref, back_out,
    spec_ref, wind_ref, coll_ref, own_table_ref, by_bin, sums, order_rows, fall_speed_ref,
    rows_got, orders, own_order, fall_ref,
    table_ref, heads, tails, from_left, from_right, picks, got, tends, cells_ref, prod_ref,
    thirds, third_left, third_on, third_right, third_sent, third_got, on_sent, on_got,
    halo_sent, halo_got, pick_sent, pick_got, back_sent, back_got, table_sent, table_got, own_sem,
    spec_sem, small_sem, rows_sent, rows_recv, orders_sem,
):
    bins, slots, nz, bx, by = spec_hbm.shape
    half = slots // 2
    ahead = half - 1
    flat = pieces(spec_ref)
    small_copies = [
        pltpu.make_async_copy(src, dst, small_sem.at[k])
        for k, (src, dst) in enumerate(
            ((order_hbm, order_rows), (order_hbm, own_order), (fall_hbm, fall_speed_ref), (wind_hbm, wind_ref), (coll_hbm, coll_ref))
        )
    ]
    for copy in small_copies[:4]:
        copy.start()

    def spec_copy(r):
        return pltpu.make_async_copy(spec_hbm.at[:, r], spec_ref.at[:, r], spec_sem.at[r])

    for r in range(slots):
        spec_copy(r).start()
    small_copies[4].start()
    blk, bin_ = lax.axis_index("blk"), lax.axis_index("bin")
    n_blk, n_bin = lax.axis_size("blk"), lax.axis_size("bin")
    share = nz // n_bin
    last = n_blk - 1
    right, left = lax.rem(blk + 1, n_blk), lax.rem(blk + last, n_blk)
    right2, left2 = lax.rem(blk + 2, n_blk), lax.rem(blk + last - 1, n_blk)
    sibling, across = bin_ + 1 - 2 * lax.rem(bin_, 2), lax.rem(bin_ + 2, n_bin)
    pair = blk + 1 - 2 * lax.rem(blk, 2)
    peers = [lax.rem(bin_ + k, n_bin) for k in range(1, n_bin)]

    barrier = pltpu.get_barrier_semaphore()
    for side in (left, right, left2, right2):
        pl.semaphore_signal(barrier, inc=1, device_id={"blk": side}, device_id_type=MESH)
    for peer in peers:
        pl.semaphore_signal(barrier, inc=1, device_id={"bin": peer}, device_id_type=MESH)
    pl.semaphore_signal(barrier, inc=1, device_id={"blk": pair, "bin": across}, device_id_type=MESH)
    pl.semaphore_wait(barrier, 5 + n_bin - 1)

    row_copies = [
        pltpu.make_async_remote_copy(
            order_rows, rows_got.at[k], rows_sent.at[k], rows_recv.at[k], device_id={"blk": side}, device_id_type=MESH
        )
        for k, side in enumerate((right, left, right2))
    ]
    small_copies[0].wait()
    for copy in row_copies:
        copy.start()
    for copy in small_copies[1:4]:
        copy.wait()

    def halos(g):
        return [
            pltpu.make_async_remote_copy(
                src.at[g], dst.at[g], halo_sent.at[k, g], halo_got.at[k, g], device_id={"blk": side}, device_id_type=MESH
            )
            for k, (src, dst, side) in enumerate(((tails, from_left, right), (heads, from_right, left)))
        ]

    def table_part(q):
        return table_ref.at[pl.ds(pl.multiple_of(q * bins, bins), bins)]

    def table_copy(k):
        src, part, peer = (
            (own_table_ref, table_part(bin_), {"bin": sibling}),
            (own_table_ref, table_part(bin_), {"blk": pair, "bin": across}),
            (table_part(across), table_part(across), {"bin": sibling}),
        )[k]
        return pltpu.make_async_remote_copy(
            src, part, table_sent.at[k], table_got.at[k], device_id=peer, device_id_type=MESH
        )

    def third_copy(r):
        return pltpu.make_async_remote_copy(
            thirds.at[r], third_left.at[r], third_sent.at[r], third_got.at[r], device_id={"blk": right}, device_id_type=MESH
        )

    def on_copy(g):
        return pltpu.make_async_remote_copy(
            third_on.at[g], third_right.at[g], on_sent.at[g], on_got.at[g], device_id={"blk": left2}, device_id_type=MESH
        )

    def pick_copies(g):
        return [
            pltpu.make_async_remote_copy(
                picks.at[g, pl.ds(peer * share, share)], got.at[bin_, g], pick_sent.at[k, g], pick_got.at[k, g],
                device_id={"bin": peer}, device_id_type=MESH,
            )
            for k, peer in enumerate(peers)
        ]

    def back_copies(g):
        return [
            pltpu.make_async_remote_copy(
                tends.at[peer, g], back_out.at[g, pl.ds(bin_ * share, share)], back_sent.at[k, g], back_got.at[k, g],
                device_id={"bin": peer}, device_id_type=MESH,
            )
            for k, peer in enumerate(peers)
        ]

    def own_back(g):
        return pltpu.make_async_copy(tends.at[bin_, g], back_out.at[g, pl.ds(bin_ * share, share)], own_sem.at[g])

    def pack(g):
        to_left, to_right = orders[0, 0, g] * nz * bx, orders[1, 0, g] * nz * bx

        def level(z, carry):
            for x in range(2):
                rows = flat[pl.ds(to_left + z * bx + x, bins, stride=slots * nz * bx), :]
                heads[g, z, x] = rows.astype(bf16)
                rows = flat[pl.ds(to_right + z * bx + bx - 2 + x, bins, stride=slots * nz * bx), :]
                tails[g, z, x] = rows.astype(bf16)
            return carry

        lax.fori_loop(0, nz, level, 0)

    def pack_third(r, carry):
        spec_copy(r).wait()

        def level(z, inner):
            low = flat[pl.ds(r * nz * bx + z * bx + 2, bins, stride=slots * nz * bx), :]
            high = flat[pl.ds(r * nz * bx + z * bx + bx - 3, bins, stride=slots * nz * bx), :]
            pos = jnp.broadcast_to(wind_ref[z, pl.ds(r, 1), :], (bins, by)) > 0
            thirds[r, z] = jnp.where(pos, high, low).astype(bf16)
            return inner

        lax.fori_loop(0, nz, level, 0)
        third_copy(r).start()
        return carry

    def pass_on(g, carry):
        row = orders[2, 0, g]
        for z in range(nz):
            third_on[g, z] = third_left[row, z]
        on_copy(g).start()
        return carry

    def pack_and_send(g, carry):
        pack(g)
        for copy in halos(g):
            copy.start()
        return carry

    lax.fori_loop(0, slots, pack_third, 0)
    for copy in row_copies:
        copy.wait_recv()
    orders_copy = pltpu.make_async_copy(rows_got, orders, orders_sem)
    orders_copy.start()
    orders_copy.wait()
    lax.fori_loop(0, ahead, pack_and_send, 0)
    for b in range(bins):
        fall_ref[b : b + 1, :] = jnp.full((1, by), fall_speed_ref[b], f32) * courant
    small_copies[4].wait()
    pair_table(coll_ref, by_bin, sums, own_table_ref)
    table_copy(0).start()
    table_copy(1).start()
    table_ref[pl.ds(pl.multiple_of(bin_ * bins, bins), bins), :] = own_table_ref[...]

    def pack_later(g, carry):
        pack(g)
        return carry

    lax.fori_loop(ahead, slots, pack_later, 0)

    def third_arrived(r, carry):
        third_copy(r).wait_recv()
        return carry

    lax.fori_loop(0, slots, third_arrived, 0)
    lax.fori_loop(0, slots, pass_on, 0)

    @pl.when(blk == 0)
    def _():
        third_left[...] = jnp.zeros(third_left.shape, bf16)

    def transport(g):
        row = own_order[0, g]
        for first in range(0, bins, 8):
            fall = fall_ref[first : first + 8, :]
            start = (first * slots + row) * nz * bx

            def level(step, above, first=first, fall=fall, start=start):
                z = nz - 1 - step
                speed = jnp.broadcast_to(wind_ref[z, pl.ds(row, 1), :], (8, by))
                pos = speed > 0
                cw = courant * jnp.abs(speed)
                own = [flat[pl.ds(start + z * bx + x, 8, stride=slots * nz * bx), :] for x in range(bx)]
                head = [from_left[g, z, x, first : first + 8, :].astype(f32) for x in range(2)]
                tail = [from_right[g, z, x, first : first + 8, :].astype(f32) for x in range(2)]
                head = [third_left[row, z, first : first + 8, :].astype(f32)] + head
                tail = tail + [third_right[g, z, first : first + 8, :].astype(f32)]
                adv = advect_cells(head + own + tail, pos, cw * 0.5, cw * (1.0 / 6.0))
                settled = jnp.stack([adv[x] - fall * (adv[x] - above[x]) for x in range(bx)])
                settled_ref[g, first : first + 8, z] = jnp.swapaxes(settled, 0, 1)

                @pl.when(g < half)
                def _():
                    for x in range(bx):
                        picks[g, z, x, first : first + 8, :] = settled[x].astype(bf16)

                return tuple(adv)

            lax.fori_loop(0, nz, level, tuple(jnp.zeros((8, by), f32) for _ in range(bx)))

    def collect(g):
        def pair(step, carry):
            zz, first = step // (bx // 2), step % (bx // 2) * 2
            for part in range(2):
                lanes = slice(part * by, (part + 1) * by)
                cells = [got[q, g, zz, first + part] for q in range(n_bin)]
                for q in range(n_bin):
                    cells_ref[q * bins : q * bins + bins, :] = cells[q].astype(f32)
                row = 0
                for i in range(n_bin * bins):
                    one = jnp.broadcast_to(cells_ref[i : i + 1, :], (bins, by)).astype(bf16)
                    for q in range(i // bins, n_bin):
                        prod_ref[row : row + bins, lanes] = one * cells[q]
                        row += bins
            total = jnp.dot(table_ref[...], prod_ref[...], preferred_element_type=f32).astype(bf16)
            for part in range(2):
                for q in range(n_bin):
                    tends[q, g, zz, first + part] = total[q * bins : q * bins + bins, part * by : (part + 1) * by]
            return carry

        lax.fori_loop(0, share * bx // 2, pair, 0)

    def slot(g, carry):
        on_copy(g).wait_recv()
        for copy in halos(g):
            copy.wait_recv()

        @pl.when(blk == 0)
        def _():
            from_left[g] = jnp.zeros(from_left.shape[1:], bf16)

        @pl.when(blk == last)
        def _():
            from_right[g] = jnp.zeros(from_right.shape[1:], bf16)
            third_right[g] = jnp.zeros(third_right.shape[1:], bf16)

        transport(g)

        @pl.when(g < half)
        def _():
            for copy in pick_copies(g):
                copy.start()
            got[bin_, g] = picks[g, pl.ds(bin_ * share, share)]

        @pl.when(g + ahead < slots)
        def _():
            for copy in halos(g + ahead):
                copy.start()

        @pl.when(g == 0)
        def _():
            table_copy(1).wait_recv()
            table_copy(2).start()

        @pl.when(g == 1)
        def _():
            table_copy(0).wait_recv()
            table_copy(2).wait_recv()

        @pl.when(jnp.logical_and(g >= 1, g <= half))
        def _():
            for copy in pick_copies(g - 1):
                copy.wait_recv()
            collect(g - 1)
            for copy in back_copies(g - 1):
                copy.start()
            own_back(g - 1).start()

        return carry

    lax.fori_loop(0, slots, slot, 0)

    for copy in row_copies + [table_copy(k) for k in range(3)]:
        copy.wait_send()

    def finish(g, carry):
        third_copy(g).wait_send()
        on_copy(g).wait_send()
        for copy in halos(g):
            copy.wait_send()
        return carry

    lax.fori_loop(0, slots, finish, 0)

    def finish_active(g, carry):
        for copy in pick_copies(g):
            copy.wait_send()
        for copy in back_copies(g):
            copy.wait()
        own_back(g).wait()
        return carry

    lax.fori_loop(0, half, finish_active, 0)


def update_body(order_ref, count_ref, settled_ref, tend_ref, out_ref, rows_ref, out_sem):
    slots = settled_ref.shape[0]
    half, bins, nz, bx, by = rows_ref.shape

    def copy(src, g):
        return pltpu.make_async_copy(src.at[g], out_ref.at[:, order_ref[g]], out_sem.at[g])

    for g in range(half, slots):
        copy(settled_ref, g).start()

    def active(g, carry):
        on = jnp.full((bins, bx, by), g, jnp.int32) < count_ref[0]

        def level(z, inner):
            add = jnp.swapaxes(tend_ref[g, z].astype(f32), 0, 1) * time_step
            rows_ref[g, :, z] = settled_ref[g, :, z] + jnp.where(on, add, 0.0)
            return inner

        lax.fori_loop(0, nz, level, 0)
        copy(rows_ref, g).start()
        return carry

    lax.fori_loop(0, half, active, 0)
    for g in range(half):
        copy(rows_ref, g).wait()
    for g in range(half, slots):
        copy(settled_ref, g).wait()


def local(spectrum, wind, fall_speed, collection, act_order, act_count):
    bins, slots, nz, bx, by = spectrum.shape
    n_blk, n_bin = lax.axis_size("blk"), lax.axis_size("bin")
    half, share, every = slots // 2, nz // n_bin, bins * n_bin
    order = act_order[0]
    pairs = sum(bins * (every - first) for first in range(0, every, bins))

    inputs = (act_order, fall_speed, spectrum, jnp.transpose(wind, (1, 0, 2)), jnp.transpose(collection, (0, 2, 1)))

    smem, vmem, hbm = (pl.BlockSpec(memory_space=s) for s in (pltpu.SMEM, pltpu.VMEM, pl.ANY))
    side = pltpu.VMEM((slots, nz, 2, bins, by), bf16)
    third = pltpu.VMEM((slots, nz, bins, by), bf16)
    dma = pltpu.SemaphoreType.DMA
    settled, back = pl.pallas_call(
        step_body,
        in_specs=[pl.BlockSpec(memory_space=pltpu.HBM)] * 5,
        out_specs=[vmem, hbm],
        out_shape=[
            jax.ShapeDtypeStruct((slots, bins, nz, bx, by), f32),
            jax.ShapeDtypeStruct((half, nz, bx, bins, by), bf16),
        ],
        scratch_shapes=[
            pltpu.VMEM(spectrum.shape, f32),
            pltpu.VMEM((nz, slots, by), f32),
            pltpu.VMEM((every, bins, every), bf16),
            pltpu.VMEM((bins, pairs), bf16),
            pltpu.VMEM((bins, every, every), f32),
            pltpu.VMEM((every, bins, every), f32),
            pltpu.VMEM((1, slots), jnp.int32),
            pltpu.SMEM((bins,), f32),
            pltpu.VMEM((3, 1, slots), jnp.int32),
            pltpu.SMEM((3, 1, slots), jnp.int32),
            pltpu.SMEM((1, slots), jnp.int32),
            pltpu.VMEM((bins, by), f32),
            pltpu.VMEM((every, pairs), bf16),
            side, side, side, side,
            pltpu.VMEM((half, nz, bx, bins, by), bf16),
            pltpu.VMEM((n_bin, half, share, bx, bins, by), bf16),
            pltpu.VMEM((n_bin, half, share, bx, bins, by), bf16),
            pltpu.VMEM((every, by), f32),
            pltpu.VMEM((pairs, 2 * by), bf16),
            third, third, third, third,
            dma((slots,)), dma((slots,)), dma((slots,)), dma((slots,)),
            dma((2, slots)), dma((2, slots)),
            dma((n_bin - 1, half)), dma((n_bin - 1, half)),
            dma((n_bin - 1, half)), dma((n_bin - 1, half)),
            dma((n_bin - 1,)), dma((n_bin - 1,)),
            dma((half,)), dma((slots,)), dma((5,)), dma((3,)), dma((3,)), dma(()),
        ],
        compiler_params=pltpu.CompilerParams(collective_id=0, has_side_effects=True, vmem_limit_bytes=42 << 20),
    )(*(pltpu.with_memory_space_constraint(a, pltpu.HBM) for a in inputs))

    return pl.pallas_call(
        update_body,
        in_specs=[smem, smem, vmem, vmem],
        out_specs=hbm,
        out_shape=jax.ShapeDtypeStruct(spectrum.shape, f32),
        scratch_shapes=[pltpu.VMEM((half, bins, nz, bx, by), f32), dma((slots,))],
        compiler_params=pltpu.CompilerParams(vmem_limit_bytes=16 << 20),
    )(order, act_count, settled, back)


def solution(mesh):
    return jax.shard_map(
        local,
        mesh=mesh,
        in_specs=(
            P("bin", None, None, "blk", None),
            P(),
            P("bin"),
            P(None, None, "bin"),
            P("blk", None),
            P("blk"),
        ),
        out_specs=P("bin", None, None, "blk", None),
        check_vma=False,
    )
```
